32 devices in a mesh: layer: 2 (over x), band: 16 (over z, y, core).
Axes of the slice: x: 2, y: 2, z: 4, core: 2. Of those that a mesh axis runs over, the one named last changes fastest.
Arguments:
- coeffs: bfloat16 [32, 128, 10240], P('layer', None, 'band'), may hold values from -6 to 6
- hamilton: bfloat16 [32, 7, 128, 128], P('layer'), may hold values from -0.1875 to 0.1875
- neighbors: int32 [32, 7], P('layer'), may hold values from -1 to 31, as said below
- basis: bfloat16 [32, 1728, 128], P(('layer', 'band')), may hold values from -0.5 to 0.5
- occupation: int32 [10240], replicated, may hold values from 0 to 3
Outputs:
- filtered: bfloat16 [32, 128, 10240], P('layer', None, 'band')
- density: float32 [32, 1728], P(('layer', 'band'))
The draws below stay inside these ranges and needn't reach their ends.
Inputs may be any that keep to these rules, and one draw needn't show every extreme that they name: `neighbors`: column 0 of row e is e itself; columns 1 to 4 are its neighbours along the two periodic in-plane directions, all in e's plane of 16 elements (rows e // 16 * 16 to that plus 16 - 1); columns 5 and 6 are the elements at the same lattice site in the previous and the next plane, -1 before the first and after the last plane. The numbering of sites within each plane is drawn.
All inputs are finite; a program needn't handle non-finite values.
Results may differ from the reference program's by a relative error of at most 0.0042.
Values may be sent and summed in bfloat16 or wider, within the bound.
A program may use at most 64 MiB of HBM per device.

```python
import jax
import jax.numpy as jnp
from jax import lax

NB = 128
NBAND = 10240
FY = 4
FZ = 4
ELEMS_DEV = 16
E = 32
GP = 1728
OWNERS = 32
N_BAND = 16


def draw_neighbors(key, part):
    face_size = FY * FZ
    planes = E // face_size
    plane_keys = jax.random.split(jax.random.fold_in(key, 17), planes)
    shuffled = jax.vmap(lambda subkey: jax.random.permutation(subkey, face_size))(plane_keys).astype(jnp.int32)
    element_at = jnp.arange(planes, dtype=jnp.int32)[:, None] * face_size + shuffled
    sites = jnp.arange(face_size, dtype=jnp.int32)
    site_y = sites // FZ
    site_z = sites % FZ
    y_minus = (site_y - 1) % FY * FZ + site_z
    y_plus = (site_y + 1) % FY * FZ + site_z
    z_minus = site_y * FZ + (site_z - 1) % FZ
    z_plus = site_y * FZ + (site_z + 1) % FZ
    missing = jnp.full((1, face_size), -1, jnp.int32)
    before = jnp.concatenate([missing, element_at[:-1]], axis=0)
    after = jnp.concatenate([element_at[1:], missing], axis=0)
    table = jnp.stack([element_at, element_at[:, y_minus], element_at[:, y_plus], element_at[:, z_minus], element_at[:, z_plus], before, after], axis=-1)
    result = jnp.zeros((E, 7), jnp.int32)
    return result.at[element_at.reshape(-1)].set(table.reshape(-1, 7))


def place_ends(array, key, smallest, top_value):
    index_at = [jax.random.randint(jax.random.fold_in(key, axis), (), 0, length) for axis, length in enumerate(array.shape)]
    main_axis = array.shape.index(max(array.shape))
    beside = index_at[:main_axis] + [(index_at[main_axis] + 1) % array.shape[main_axis]] + index_at[main_axis + 1:]
    return array.at[tuple(index_at)].set(smallest).at[tuple(beside)].set(top_value)


def steps_of(key, shape, cuts, low, top_value):
    loudness, own = 1.0, jax.random.fold_in(key, 6)
    for dim, blocks in cuts:
        heights = jnp.exp(jax.random.uniform(jax.random.fold_in(own, dim), (blocks,), jnp.float32, low / len(cuts), top_value / len(cuts)))
        loudness = loudness * jnp.repeat(heights, shape[dim] // blocks).reshape([-1 if axis == dim else 1 for axis in range(len(shape))])
    return loudness


def noise(key, shape, scale, most, pieces=(), kind=jnp.bfloat16):
    values = scale * jax.random.normal(key, shape, jnp.float32)
    if pieces:
        values = values * steps_of(key, shape, pieces, -0.22, 0.18)
    return jnp.clip(values, -most, most).astype(kind)


def setup_inputs(seed: int = 0) -> dict:
    seeds = jax.random.split(jax.random.key(seed), 6)
    coeffs = noise(seeds[0], (E, NB, NBAND), 1.0, 6.0, ((0, 2), (2, 16)))
    hamilton = noise(seeds[1], (E, 7, NB, NB), (7 * NB) ** -0.5, 0.1875, ((0, 2),))
    neighbors = draw_neighbors(jax.random.fold_in(seeds[5], 71), 0)
    basis = noise(seeds[3], (OWNERS, GP, NB), NB ** -0.5, 0.5, ((0, 32),))
    occupation = place_ends(jax.random.randint(seeds[4], (NBAND,), 0, 4), jax.random.fold_in(seeds[4], 1), 0, 3).astype(jnp.int32)
    return dict(coeffs=coeffs, hamilton=hamilton, neighbors=neighbors, basis=basis, occupation=occupation)


center = 0.5
half_width = 1.5


def apply_hamiltonian(source, hamilton, neighbors):
    usable = neighbors >= 0
    clipped = jnp.where(usable, neighbors, 0).astype(jnp.int32)

    def one_row(packed):
        blocks, lookup, allowed = packed
        nearby = source[lookup].astype(jnp.float32) * allowed.astype(jnp.float32)[:, None, None]
        return jnp.einsum("kij,kjb->ib", blocks.astype(jnp.float32), nearby)

    return lax.map(one_row, (hamilton, clipped, usable))


def reference(coeffs, hamilton, neighbors, basis, occupation):
    start_vals = coeffs.astype(jnp.float32)
    first_image = apply_hamiltonian(coeffs, hamilton, neighbors)
    filtered_once = ((first_image - center * start_vals) / half_width).astype(jnp.bfloat16)
    second_image = apply_hamiltonian(filtered_once, hamilton, neighbors)
    filtered = (2.0 * (second_image - center * filtered_once.astype(jnp.float32)) / half_width - start_vals).astype(jnp.bfloat16)
    weights = (1 + occupation).astype(jnp.float32) / (2.0 * NBAND)

    def owner_density(owner_id):
        layer_pos = owner_id // N_BAND
        band_pos = owner_id % N_BAND
        element = (layer_pos * ELEMS_DEV + band_pos % ELEMS_DEV).astype(jnp.int32)
        orbital = jnp.dot(basis[owner_id], filtered[element], preferred_element_type=jnp.float32)
        return jnp.sum(orbital * orbital * weights[None, :], axis=1)

    density = lax.map(owner_density, jnp.arange(OWNERS, dtype=jnp.int32))
    return filtered, density
```

```python
import functools

import jax
import jax.numpy as jnp
from jax import lax
from jax.experimental import pallas as pl
from jax.experimental.pallas import tpu as pltpu
from jax.sharding import PartitionSpec as P

FY = 4
FZ = 4
MESH = pl.DeviceIdType.MESH

center = 0.5
half_width = 1.5


def with_halo(array, sides, width):
    for axis, dim in sides:
        devices, length = (lax.axis_size(axis), array.shape[dim])
        up = [(i, (i + 1) % devices) for i in range(devices - 1)]
        down = [(j, i) for i, j in up]
        last = lax.slice_in_dim(array, length - width, length, axis=dim)
        first = lax.slice_in_dim(array, 0, width, axis=dim)
        before = lax.ppermute(last, axis, up)
        after = lax.ppermute(first, axis, down)
        array = jnp.concatenate([before, array, after], axis=dim)
    return array


def neighbor_product(blocks, nearby):
    return jnp.einsum("ekij,ekjb->eib", blocks, nearby, preferred_element_type=jnp.float32)


def general_body(coeffs, hamilton, neighbors, basis, occupation):
    elements = coeffs.shape[0]
    face_size = FY * FZ
    offset = lax.axis_index("layer") * elements - face_size
    usable = neighbors >= 0
    position = jnp.where(usable, neighbors - offset, 0)
    allowed = usable.astype(jnp.bfloat16)

    def operate(source):
        padded = with_halo(source, (("layer", 0),), face_size)
        inside = source[position[:, :5] - face_size]
        result = neighbor_product(hamilton[:, :5], inside)
        across = padded[position[:, 5:]] * allowed[:, 5:, None, None]
        return result + neighbor_product(hamilton[:, 5:], across)

    start_vals = coeffs.astype(jnp.float32)
    first_image = operate(coeffs)
    filtered_once = ((first_image - center * start_vals) / half_width).astype(jnp.bfloat16)
    second_image = operate(filtered_once)
    filtered = (
        2.0 * (second_image - center * filtered_once.astype(jnp.float32)) / half_width - start_vals
    ).astype(jnp.bfloat16)
    weights = (1 + occupation).astype(jnp.float32) / (2.0 * occupation.shape[0])
    copies = lax.axis_size("band") // elements
    duplicated = jnp.tile(filtered, (copies, 1, 1))
    regrouped = lax.all_to_all(duplicated, "band", split_axis=0, concat_axis=2, tiled=True)
    orbital = jnp.dot(basis[0], regrouped[0], preferred_element_type=jnp.float32)
    density = jnp.sum(orbital * orbital * weights[None, :], axis=1)[None, :]
    return (filtered, density)


def kernel(nb, n, c_hbm, h_hbm, nbr_hbm, occ_hbm, basis_hbm, out_ref, dens_ref, *scratch):
    elements, _, nbl = c_hbm.shape
    count = nbl // n
    cown, cx = scratch[:count], scratch[count:2 * count]
    (f1o, f1x, hown, hx, nx_v, nown, nx, occ_v, functions, gram, across,
     gsend_a, gcore_a, grecv_a, gsend_b, gcore_b, grecv_b, total_out, total_in,
     c_send, c_recv, hx_send, hx_recv, n_send, n_recv, f_send, f_recv,
     ka_send, ka_recv, ga_send, ga_recv, kb_send, kb_recv, gb_send, gb_recv, t_send, t_recv,
     lc_sem, lh_sem, misc_sem, x_ready, all_in) = scratch[2 * count:]
    layer, b = lax.axis_index("layer"), lax.axis_index("band")
    other = 1 - layer
    nz = nb // 4
    half = nb // 2
    site = b // 2
    z, y, core = b // 4, (b // 2) % 2, b % 2
    core_peer = b + 1 - 2 * core
    own_cross, x_cross = 6 - layer, 6 - other
    last = count - 1

    def ident(zz, yy, cc):
        return zz * 4 + yy * 2 + cc

    def place(s, side=layer):
        return pl.multiple_of((s + side * (last - 2 * s)) * n, n)

    barrier = pltpu.get_barrier_semaphore()

    @pl.when(layer == 0)
    def _():
        pl.semaphore_signal(barrier, inc=1, device_id={"layer": other, "band": b}, device_id_type=MESH)

    @pl.when(layer == 1)
    def _():
        pl.semaphore_wait(barrier, 1)
        pl.semaphore_signal(x_ready, inc=1, device_id={"layer": other, "band": b}, device_id_type=MESH)

    @pl.when(layer == 0)
    def _():
        pl.semaphore_wait(x_ready, 1)

    def to_x(src, dst, send, recv):
        return pltpu.make_async_remote_copy(
            src_ref=src, dst_ref=dst, send_sem=send, recv_sem=recv,
            device_id={"layer": other, "band": b}, device_id_type=MESH)

    def to_band(src, dst, send, recv, peer):
        return pltpu.make_async_remote_copy(
            src_ref=src, dst_ref=dst, send_sem=send, recv_sem=recv,
            device_id={"layer": layer, "band": peer}, device_id_type=MESH)

    h_across = [
        to_x(h_hbm.at[b, pl.ds(0, 5)], hx.at[b, pl.ds(0, 5)], hx_send.at[0], hx_recv.at[0]),
        to_x(h_hbm.at[b, pl.ds(own_cross, 1)], hx.at[b, pl.ds(5, 1)], hx_send.at[1], hx_recv.at[1]),
    ]
    n_across = to_x(nbr_hbm, nx_v, n_send.at[0], n_recv.at[0])
    c_across = [
        to_x(c_hbm.at[:, :, pl.ds(place(s, other), n)], cx[s], c_send.at[s], c_recv.at[s]) for s in range(count)
    ]
    for copy in h_across + [n_across] + c_across[:last]:
        copy.start()

    n_copy = pltpu.make_async_copy(nbr_hbm, nown, misc_sem.at[0])
    occ_copy = pltpu.make_async_copy(occ_hbm.at[:, pl.ds(pl.multiple_of(b * nbl, n), nbl)], occ_v, misc_sem.at[2])
    basis_copy = pltpu.make_async_copy(basis_hbm.at[0], functions, misc_sem.at[3])
    h_copies = [
        pltpu.make_async_copy(h_hbm.at[:, pl.ds(0, 5)], hown.at[:, pl.ds(0, 5)], lh_sem.at[0]),
        pltpu.make_async_copy(h_hbm.at[:, pl.ds(own_cross, 1)], hown.at[:, pl.ds(5, 1)], lh_sem.at[1]),
    ]
    c_copies = [
        pltpu.make_async_copy(c_hbm.at[:, :, pl.ds(place(s), n)], cown[s], lc_sem.at[s]) for s in range(count)
    ]
    for copy in [n_copy, occ_copy] + h_copies + c_copies + [basis_copy]:
        copy.start()

    @pl.when(layer == 0)
    def _():
        for peer in [core_peer] + [(site + k) % half * 2 + core for k in range(1, half)]:
            pl.semaphore_signal(barrier, inc=1, device_id={"layer": layer, "band": peer}, device_id_type=MESH)
        pl.semaphore_wait(barrier, half)
        pl.semaphore_signal(all_in, inc=1, device_id={"layer": other, "band": b}, device_id_type=MESH)

    @pl.when(layer == 1)
    def _():
        pl.semaphore_wait(all_in, 1)

    sent = []

    def forward(block, peer):
        slot = len(sent)
        copy = to_band(hx.at[block], hx.at[block], f_send.at[slot], f_recv.at[block], peer)
        copy.start()
        sent.append(copy)

    def arrived(block, peer):
        to_band(hx.at[block], hx.at[block], f_send.at[0], f_recv.at[block], peer).wait_recv()

    y_peer = ident(z, 1 - y, core)
    for copy in h_across:
        copy.wait_recv()
    for k in range(1, nz):
        forward(b, ident((z + k) % nz, y, core))
    forward(b, y_peer)
    forward(b, core_peer)
    for k in range(1, nz):
        block = ident((z - k + nz) % nz, y, core)
        arrived(block, block)
        forward(block, y_peer)
        forward(block, core_peer)
    for k in range(nz):
        block = ident((z - k + nz) % nz, 1 - y, core)
        arrived(block, y_peer)
        forward(block, core_peer)
    for k in range(nz):
        for yy in (y, 1 - y):
            arrived(ident((z - k + nz) % nz, yy, 1 - core), core_peer)

    n_across.wait_recv()
    nx_copy = pltpu.make_async_copy(nx_v, nx, misc_sem.at[1])
    nx_copy.start()
    for copy in [n_copy, nx_copy, occ_copy] + h_copies:
        copy.wait()

    def image(blocks, table, e, cross, near, far):
        row = jnp.concatenate([blocks[e, k] for k in range(6)], axis=1)
        parts = [near[lax.rem(table[k, e], elements)] for k in range(5)]
        parts.append(far[lax.rem(table[cross, e], elements)])
        return jnp.dot(row, jnp.concatenate(parts, axis=0), preferred_element_type=jnp.float32)

    def once(got, start):
        return ((got - center * start.astype(jnp.float32)) * (1.0 / half_width)).astype(jnp.bfloat16)

    def twice(got, middle, start):
        value = (got - center * middle.astype(jnp.float32)) * (2.0 / half_width) - start.astype(jnp.float32)
        return value.astype(jnp.bfloat16)

    def square(value, weight):
        scaled = (value.astype(jnp.float32) * weight).astype(jnp.bfloat16)
        return lax.dot_general(scaled, value, (((1,), (1,)), ((), ())), preferred_element_type=jnp.float32)

    def pairs(body):
        def both(t, carry):
            body([2 * t, 2 * t + 1])
            return carry
        lax.fori_loop(0, elements // 2, both, 0)

    def filter_chunk(s):
        c_copies[s].wait()
        c_across[s].wait_recv()
        own, far = cown[s], cx[s]
        weight = (1 + occ_v[:, pl.ds(place(s), n)]).astype(jnp.float32)

        def first(at):
            mine = [once(image(hown, nown, e, own_cross, own, far), own[e]) for e in at]
            theirs = [once(image(hx, nx, e, x_cross, far, own), far[e]) for e in at]
            for e, a, c in zip(at, mine, theirs):
                f1o[e] = a
                f1x[e] = c

        def second(at):
            got = [twice(image(hown, nown, e, own_cross, f1o, f1x), f1o[e], own[e]) for e in at]
            if s < last:
                parts = [square(value, weight) for value in got]
                if s > 0:
                    parts = [part + gram[e] for e, part in zip(at, parts)]
                for e, part in zip(at, parts):
                    gram[e] = part
            for e, value in zip(at, got):
                out_ref[e, :, pl.ds(place(s), n)] = value

        def second_x(at):
            got = [twice(image(hx, nx, e, x_cross, f1x, f1o), f1x[e], far[e]) for e in at]
            for e, part in zip(at, [square(value, weight) for value in got]):
                across[e] = part

        pairs(first)
        pairs(second)
        if s == 0:
            pairs(second_x)

    def reduction(source, gsend, gcore, grecv, k_send, k_recv, g_send, g_recv):
        def to_core(t):
            return to_band(gsend.at[2 * t + 1 - core], gcore.at[t], k_send.at[t], k_recv.at[t], core_peer)

        def to_owner(k):
            element = (site + k) % half * 2 + core
            return to_band(gsend.at[element], grecv.at[k], g_send.at[k], g_recv.at[k], element)

        def pair_up(t, carry):
            gsend[2 * t + 1 - core] = source[2 * t + 1 - core].astype(jnp.bfloat16)
            to_core(t).start()
            return carry

        def hand_over(i, carry):
            k = i + 1
            t = (site + k) % half
            to_core(t).wait_recv()
            gsend[2 * t + core] = (source[2 * t + core] + gcore[t].astype(jnp.float32)).astype(jnp.bfloat16)
            to_owner(k).start()
            return carry

        def begin():
            lax.fori_loop(0, half, pair_up, 0)
            lax.fori_loop(0, half - 1, hand_over, 0)

        def end():
            to_core(site).wait_recv()
            total = source[b] + gcore[site].astype(jnp.float32)
            for k in range(1, half):
                to_owner(k).wait_recv()
                total = total + grecv[k].astype(jnp.float32)
            return total

        def drain():
            for t in range(half):
                to_core(t).wait_send()
            for k in range(1, half):
                to_owner(k).wait_send()

        return begin, end, drain

    begin_a, end_a, drain_a = reduction(across, gsend_a, gcore_a, grecv_a, ka_send, ka_recv, ga_send, ga_recv)
    begin_b, end_b, drain_b = reduction(gram, gsend_b, gcore_b, grecv_b, kb_send, kb_recv, gb_send, gb_recv)
    t_across = to_x(total_out, total_in, t_send.at[0], t_recv.at[0])

    filter_chunk(0)
    begin_a()
    for s in range(1, last):
        if s > 1:
            filter_chunk(s)
            continue
        filter_chunk(s)
        total_out[...] = end_a().astype(jnp.bfloat16)
        t_across.start()
        c_across[last].start()
    begin_b()
    total = end_b()
    t_across.wait_recv()
    total = (total + total_in[...].astype(jnp.float32)) * (1.0 / (2.0 * nbl * nb))

    high = total.astype(jnp.bfloat16)
    low = (total - high.astype(jnp.float32)).astype(jnp.bfloat16)
    basis_copy.wait()
    values = functions[...]
    image_g = jnp.dot(values, high, preferred_element_type=jnp.float32)
    image_g = image_g + jnp.dot(values, low, preferred_element_type=jnp.float32)
    product = image_g * values.astype(jnp.float32)
    top = product.astype(jnp.bfloat16)
    rest = (product - top.astype(jnp.float32)).astype(jnp.bfloat16)
    ones = jnp.ones((16, product.shape[1]), jnp.bfloat16)
    over_last = (((1,), (1,)), ((), ()))
    density = lax.dot_general(ones, top, over_last, preferred_element_type=jnp.float32)
    density = density + lax.dot_general(ones, rest, over_last, preferred_element_type=jnp.float32)
    dens_ref[...] = density[0:1]

    filter_chunk(last)

    for copy in h_across + [n_across, t_across] + c_across + sent:
        copy.wait_send()
    drain_a()
    drain_b()


def plane_body(nb, coeffs, hamilton, neighbors, basis, occupation):
    elements, nbasis, nbl = coeffs.shape
    points = basis.shape[1]
    n = 128
    count = nbl // n
    width = neighbors.shape[1]
    half = nb // 2
    dma = pltpu.SemaphoreType.DMA
    hbm = pl.BlockSpec(memory_space=pl.ANY)
    vmem = pl.BlockSpec(memory_space=pltpu.VMEM)
    forwards = (nb // 4 - 1) + 2 + 2 * (nb // 4 - 1) + nb // 4
    bf16, f32 = jnp.bfloat16, jnp.float32
    chunk = pltpu.VMEM((elements, nbasis, n), bf16)
    rounds = [
        pltpu.VMEM((elements, nbasis, nbasis), bf16),
        pltpu.VMEM((half, nbasis, nbasis), bf16),
        pltpu.VMEM((half, nbasis, nbasis), bf16),
    ]
    operands = [coeffs, hamilton, neighbors.T, occupation.reshape(1, -1), basis]
    operands = [pltpu.with_memory_space_constraint(x, pltpu.HBM) for x in operands]
    return pl.pallas_call(
        functools.partial(kernel, nb, n),
        out_shape=(
            jax.ShapeDtypeStruct(coeffs.shape, bf16),
            jax.ShapeDtypeStruct((1, points), f32),
        ),
        in_specs=[hbm] * 5,
        out_specs=(vmem, vmem),
        scratch_shapes=[chunk] * (2 * count) + [
            chunk, chunk,
            pltpu.VMEM((elements, 6, nbasis, nbasis), bf16),
            pltpu.VMEM((elements, 6, nbasis, nbasis), bf16),
            pltpu.VMEM((width, elements), jnp.int32),
            pltpu.SMEM((width, elements), jnp.int32),
            pltpu.SMEM((width, elements), jnp.int32),
            pltpu.VMEM((1, nbl), jnp.int32),
            pltpu.VMEM((points, nbasis), bf16),
            pltpu.VMEM((elements, nbasis, nbasis), f32),
            pltpu.VMEM((elements, nbasis, nbasis), f32),
        ] + rounds + rounds + [
            pltpu.VMEM((nbasis, nbasis), bf16),
            pltpu.VMEM((nbasis, nbasis), bf16),
            dma((count,)), dma((count,)),
            dma((2,)), dma((2,)),
            dma((1,)), dma((1,)),
            dma((forwards,)), dma((nb,)),
        ] + [dma((half,))] * 8 + [
            dma((1,)), dma((1,)),
            dma((count,)), dma((2,)), dma((4,)),
            pltpu.SemaphoreType.REGULAR, pltpu.SemaphoreType.REGULAR,
        ],
        compiler_params=pltpu.CompilerParams(
            collective_id=0, has_side_effects=True, vmem_limit_bytes=40 * 2**20),
    )(*operands)


def solution(mesh):
    layers, nb = mesh.shape["layer"], mesh.shape["band"]

    def body(coeffs, hamilton, neighbors, basis, occupation):
        elements = coeffs.shape[0]
        one_kernel = (
            layers == 2 and elements == FY * FZ and nb == elements
            and nb % 4 == 0 and nb >= 8 and coeffs.shape[2] % 128 == 0 and coeffs.shape[2] >= 512
            and coeffs.shape[1] == 128 and basis.shape[0] == 1
        )
        if one_kernel:
            return plane_body(nb, coeffs, hamilton, neighbors, basis, occupation)
        return general_body(coeffs, hamilton, neighbors, basis, occupation)

    return jax.shard_map(
        body,
        mesh=mesh,
        in_specs=(
            P("layer", None, "band"),
            P("layer", None, None, None),
            P("layer", None),
            P(("layer", "band"), None, None),
            P(),
        ),
        out_specs=(P("layer", None, "band"), P(("layer", "band"), None)),
        check_vma=False,
    )
```

```python
import functools

import jax
import jax.numpy as jnp
from jax import lax
from jax.experimental import pallas as pl
from jax.experimental.pallas import tpu as pltpu
from jax.sharding import PartitionSpec as P

FY = 4
FZ = 4
MESH = pl.DeviceIdType.MESH

center = 0.5
half_width = 1.5


def with_halo(array, sides, width):
    for axis, dim in sides:
        devices, length = (lax.axis_size(axis), array.shape[dim])
        up = [(i, (i + 1) % devices) for i in range(devices - 1)]
        down = [(j, i) for i, j in up]
        last = lax.slice_in_dim(array, length - width, length, axis=dim)
        first = lax.slice_in_dim(array, 0, width, axis=dim)
        before = lax.ppermute(last, axis, up)
        after = lax.ppermute(first, axis, down)
        array = jnp.concatenate([before, array, after], axis=dim)
    return array


def neighbor_product(blocks, nearby):
    return jnp.einsum("ekij,ekjb->eib", blocks, nearby, preferred_element_type=jnp.float32)


def general_body(coeffs, hamilton, neighbors, basis, occupation):
    elements = coeffs.shape[0]
    face_size = FY * FZ
    offset = lax.axis_index("layer") * elements - face_size
    usable = neighbors >= 0
    position = jnp.where(usable, neighbors - offset, 0)
    allowed = usable.astype(jnp.bfloat16)

    def operate(source):
        padded = with_halo(source, (("layer", 0),), face_size)
        inside = source[position[:, :5] - face_size]
        result = neighbor_product(hamilton[:, :5], inside)
        across = padded[position[:, 5:]] * allowed[:, 5:, None, None]
        return result + neighbor_product(hamilton[:, 5:], across)

    start_vals = coeffs.astype(jnp.float32)
    first_image = operate(coeffs)
    filtered_once = ((first_image - center * start_vals) / half_width).astype(jnp.bfloat16)
    second_image = operate(filtered_once)
    filtered = (
        2.0 * (second_image - center * filtered_once.astype(jnp.float32)) / half_width - start_vals
    ).astype(jnp.bfloat16)
    weights = (1 + occupation).astype(jnp.float32) / (2.0 * occupation.shape[0])
    copies = lax.axis_size("band") // elements
    duplicated = jnp.tile(filtered, (copies, 1, 1))
    regrouped = lax.all_to_all(duplicated, "band", split_axis=0, concat_axis=2, tiled=True)
    orbital = jnp.dot(basis[0], regrouped[0], preferred_element_type=jnp.float32)
    density = jnp.sum(orbital * orbital * weights[None, :], axis=1)[None, :]
    return (filtered, density)


def kernel(nb, n, c_hbm, h_hbm, nbr_hbm, occ_hbm, basis_hbm, out_ref, dens_ref, *scratch):
    elements, nbasis, nbl = c_hbm.shape
    cx, cl = scratch[:3], scratch[3:5]
    (cown, ahead, f1o, f1x, hown, hx, nx_v, nown, nx, occ_v, functions, gram, across, row_a, row_b, base,
     gsend_a, gcore_a, grecv_a, gsend_b, gcore_b, grecv_b, total_out, total_in,
     c_send, c_recv, hx_send, hx_recv, n_send, n_recv, f_send, f_recv,
     ka_send, ka_recv, ga_send, ga_recv, kb_send, kb_recv, gb_send, gb_recv, t_send, t_recv,
     lc_sem, lh_sem, misc_sem, x_ready, all_in) = scratch[5:]
    layer, b = lax.axis_index("layer"), lax.axis_index("band")
    other = 1 - layer
    nz = nb // 4
    half = nb // 2
    site = b // 2
    z, y, core = b // 4, (b // 2) % 2, b % 2
    core_peer = b + 1 - 2 * core
    own_cross, x_cross = 6 - layer, 6 - other
    part = nbasis // 2
    widths = (2 * n, n, n, n)
    starts = (0, 2 * n, 3 * n, 4 * n)

    def ident(zz, yy, cc):
        return zz * 4 + yy * 2 + cc

    def place(s, side=layer):
        return pl.multiple_of(starts[s] + side * (nbl - widths[s] - 2 * starts[s]), n)

    barrier = pltpu.get_barrier_semaphore()

    @pl.when(layer == 0)
    def _():
        pl.semaphore_signal(barrier, inc=1, device_id={"layer": other, "band": b}, device_id_type=MESH)

    @pl.when(layer == 1)
    def _():
        pl.semaphore_wait(barrier, 1)
        pl.semaphore_signal(x_ready, inc=1, device_id={"layer": other, "band": b}, device_id_type=MESH)

    @pl.when(layer == 0)
    def _():
        pl.semaphore_wait(x_ready, 1)

    def to_x(src, dst, send, recv):
        return pltpu.make_async_remote_copy(
            src_ref=src, dst_ref=dst, send_sem=send, recv_sem=recv,
            device_id={"layer": other, "band": b}, device_id_type=MESH)

    def to_band(src, dst, send, recv, peer):
        return pltpu.make_async_remote_copy(
            src_ref=src, dst_ref=dst, send_sem=send, recv_sem=recv,
            device_id={"layer": layer, "band": peer}, device_id_type=MESH)

    pieces = ((0, 3), (3, 3))
    h_across = [
        to_x(h_hbm.at[b, pl.ds(0, 3)], hx.at[b, pl.ds(0, 3)], hx_send.at[0], hx_recv.at[0]),
        to_x(h_hbm.at[b, pl.ds(3, 2)], hx.at[b, pl.ds(3, 2)], hx_send.at[1], hx_recv.at[1]),
        to_x(h_hbm.at[b, pl.ds(own_cross, 1)], hx.at[b, pl.ds(5, 1)], hx_send.at[2], hx_recv.at[2]),
    ]
    n_across = to_x(nbr_hbm, nx_v, n_send.at[0], n_recv.at[0])
    c_across = [
        to_x(c_hbm.at[:, :, pl.ds(place(s, other), widths[s])], cx[s], c_send.at[s], c_recv.at[s]) for s in range(3)
    ] + [
        to_x(c_hbm.at[:, pl.ds(i * part, part), pl.ds(place(3, other), n)], cl[i], c_send.at[3 + i], c_recv.at[3 + i])
        for i in range(2)
    ]
    for copy in h_across + [n_across] + c_across[:4]:
        copy.start()

    n_copy = pltpu.make_async_copy(nbr_hbm, nown, misc_sem.at[0])
    occ_copy = pltpu.make_async_copy(occ_hbm.at[:, pl.ds(pl.multiple_of(b * nbl, n), nbl)], occ_v, misc_sem.at[2])
    basis_copy = pltpu.make_async_copy(basis_hbm.at[0], functions, misc_sem.at[3])
    h_copies = [
        pltpu.make_async_copy(h_hbm.at[:, pl.ds(0, 5)], hown.at[:, pl.ds(0, 5)], lh_sem.at[0]),
        pltpu.make_async_copy(h_hbm.at[:, pl.ds(own_cross, 1)], hown.at[:, pl.ds(5, 1)], lh_sem.at[1]),
    ]
    c_copy = pltpu.make_async_copy(c_hbm, cown, lc_sem.at[0])
    for copy in [n_copy, occ_copy, c_copy] + h_copies + [basis_copy]:
        copy.start()

    @pl.when(layer == 0)
    def _():
        for peer in [core_peer] + [(site + k) % half * 2 + core for k in range(1, half)]:
            pl.semaphore_signal(barrier, inc=1, device_id={"layer": layer, "band": peer}, device_id_type=MESH)
        pl.semaphore_wait(barrier, half)
        pl.semaphore_signal(all_in, inc=1, device_id={"layer": other, "band": b}, device_id_type=MESH)

    @pl.when(layer == 1)
    def _():
        pl.semaphore_wait(all_in, 1)

    def pairs(body):
        def both(t, carry):
            body([2 * t, 2 * t + 1])
            return carry
        lax.fori_loop(0, elements // 2, both, 0)

    for copy in [n_copy, c_copy] + h_copies:
        copy.wait()

    def in_plane(at):
        def one(e):
            row = jnp.concatenate([hown[e, k] for k in range(5)], axis=1)
            parts = jnp.concatenate([cown[lax.rem(nown[k, e], elements)] for k in range(5)], axis=0)
            return jnp.dot(row, parts, preferred_element_type=jnp.float32) - center * cown[e].astype(jnp.float32)
        for e, value in zip(at, [one(e) for e in at]):
            ahead[e] = value

    pairs(in_plane)

    sent = []

    def always(body):
        body()

    def forward(block, i, peer, when=always):
        slot = len(sent)
        at, size = pieces[i]
        held = hx.at[block, pl.ds(at, size)]
        copy = to_band(held, held, f_send.at[slot], f_recv.at[block * 2 + i], peer)
        sent.append((when, copy))
        when(copy.start)

    def arrived(block, i, peer):
        at, size = pieces[i]
        held = hx.at[block, pl.ds(at, size)]
        to_band(held, held, f_send.at[0], f_recv.at[block * 2 + i], peer).wait_recv()

    def inside(zz):
        return pl.when(jnp.logical_and(zz >= 0, zz < nz))

    def both_inside(za, zb):
        return pl.when(jnp.logical_and(jnp.minimum(za, zb) >= 0, jnp.maximum(za, zb) < nz))

    y_peer = ident(z, 1 - y, core)
    for i in range(2):
        h_across[i].wait_recv()
        if i == 1:
            h_across[2].wait_recv()
        for step in (1, -1):
            forward(b, i, ident(z + step, y, core), inside(z + step))
        forward(b, i, y_peer)
        forward(b, i, core_peer)

    def over_y(away):
        for i in range(2):
            for step in (1, -1) if away else (1,):
                from_z = z - step * away
                block = ident(from_z, 1 - y, core)
                if away:
                    inside(from_z)(functools.partial(arrived, block, i, y_peer))
                    forward(block, i, core_peer, inside(from_z))
                else:
                    arrived(block, i, y_peer)
                    forward(block, i, core_peer)

    for away in range(1, nz):
        for i in range(2):
            for step in (1, -1):
                from_z = z - step * away
                block = ident(from_z, y, core)
                inside(from_z)(functools.partial(arrived, block, i, ident(z - step, y, core)))
                forward(block, i, ident(z + step, y, core), both_inside(from_z, z + step))
                forward(block, i, y_peer, inside(from_z))
                forward(block, i, core_peer, inside(from_z))
        over_y(away - 1)
    over_y(nz - 1)
    for zz in range(nz):
        for yy in range(2):
            for i in range(2):
                arrived(ident(zz, yy, 1 - core), i, core_peer)

    n_across.wait_recv()
    nx_copy = pltpu.make_async_copy(nx_v, nx, misc_sem.at[1])
    nx_copy.start()
    for copy in [nx_copy, occ_copy]:
        copy.wait()

    def image(blocks, table, e, cross, near, far):
        row = jnp.concatenate([blocks[e, k] for k in range(6)], axis=1)
        parts = [near(lax.rem(table[k, e], elements)) for k in range(5)]
        parts.append(far(lax.rem(table[cross, e], elements)))
        return jnp.dot(row, jnp.concatenate(parts, axis=0), preferred_element_type=jnp.float32)

    def once(got):
        return (got * (1.0 / half_width)).astype(jnp.bfloat16)

    def twice(got, middle, start):
        return (got - center * middle.astype(jnp.float32)) * (2.0 / half_width) - start.astype(jnp.float32)

    def square(value, weight):
        scaled = (value.astype(jnp.float32) * weight).astype(jnp.bfloat16)
        return lax.dot_general(scaled, value, (((1,), (1,)), ((), ())), preferred_element_type=jnp.float32)

    def filter_chunk(s):
        c_across[s].wait_recv()
        width = widths[s]
        columns = pl.ds(place(s), width)
        lanes = pl.ds(0, width)
        weight = (1 + occ_v[:, columns]).astype(jnp.float32)

        def own(e):
            return cown[e, :, columns]

        def far(e):
            return cx[s][e]

        def mine(e):
            return f1o[e, :, lanes]

        def theirs(e):
            return f1x[e, :, lanes]

        def first(at):
            across_x = [jnp.dot(hown[e, 5], far(lax.rem(nown[own_cross, e], elements)), preferred_element_type=jnp.float32)
                        for e in at]
            left = [once(ahead[e, :, columns] + got) for e, got in zip(at, across_x)]
            right = [once(image(hx, nx, e, x_cross, far, own) - center * far(e).astype(jnp.float32)) for e in at]
            for e, p, q in zip(at, left, right):
                f1o[e, :, lanes] = p
                f1x[e, :, lanes] = q

        def second(at):
            got = [twice(image(hown, nown, e, own_cross, mine, theirs), mine(e), own(e)).astype(jnp.bfloat16) for e in at]
            if s < 2:
                sums = [square(value, weight) for value in got]
                if s > 0:
                    sums = [added + gram[e] for e, added in zip(at, sums)]
                for e, added in zip(at, sums):
                    gram[e] = added
            for e, value in zip(at, got):
                out_ref[e, :, columns] = value

        def second_x(at):
            got = [twice(image(hx, nx, e, x_cross, theirs, mine), theirs(e), far(e)).astype(jnp.bfloat16) for e in at]
            for e, added in zip(at, [square(value, weight) for value in got]):
                across[e] = added

        pairs(first)
        if s == 0:
            pairs(second_x)
        pairs(second)

    last_columns = pl.ds(place(3), n)

    def compose(at):
        def one(e, k):
            there = lax.rem(nown[own_cross, e], elements)
            beside = lax.rem(nown[k, e], elements)
            if k == 0:
                which = 0
            else:
                target = lax.rem(nown[own_cross, beside], elements)
                which = 0
                for j in range(1, 5):
                    which = jnp.where(lax.rem(nx[j, there], elements) == target, j, which)
            row = jnp.concatenate([hown[e, k], hown[e, 5]], axis=1)
            parts = jnp.concatenate([hown[beside, 5], hx[there, which]], axis=0)
            got = jnp.dot(row, parts, preferred_element_type=jnp.float32)
            if k == 0:
                got = got - (2.0 * center) * hown[e, 5].astype(jnp.float32)
            return (got * (2.0 / half_width / half_width)).astype(jnp.bfloat16)
        rows = [[one(e, k) for k in range(5)] for e in at]
        for e, row in zip(at, rows):
            row_a[e] = jnp.concatenate([block[:, :part] for block in row], axis=1)
            row_b[e] = jnp.concatenate([block[:, part:] for block in row], axis=1)

    def own_part():
        def own(e):
            return cown[e, :, last_columns]

        def mine(e):
            return f1o[e, :, pl.ds(0, n)]

        def theirs(e):
            return f1x[e, :, pl.ds(0, n)]

        def first(at):
            left = [once(ahead[e, :, last_columns]) for e in at]
            right = [once(jnp.dot(hx[e, 5], own(lax.rem(nx[x_cross, e], elements)), preferred_element_type=jnp.float32))
                     for e in at]
            for e, p, q in zip(at, left, right):
                f1o[e, :, pl.ds(0, n)] = p
                f1x[e, :, pl.ds(0, n)] = q

        def second(at):
            got = [twice(image(hown, nown, e, own_cross, mine, theirs), mine(e), own(e)) for e in at]
            for e, value in zip(at, got):
                base[e] = value

        pairs(first)
        pairs(second)

    def far_part(row, held, e):
        parts = [held[lax.rem(nown[own_cross, lax.rem(nown[k, e], elements)], elements)] for k in range(5)]
        return base[e] + jnp.dot(row[e], jnp.concatenate(parts, axis=0), preferred_element_type=jnp.float32)

    def far_first(at):
        for e, value in zip(at, [far_part(row_a, cl[0], e) for e in at]):
            base[e] = value

    def far_last(at):
        for e, value in zip(at, [far_part(row_b, cl[1], e) for e in at]):
            out_ref[e, :, last_columns] = value.astype(jnp.bfloat16)

    def reduction(source, gsend, gcore, grecv, k_send, k_recv, g_send, g_recv):
        def to_core(t):
            return to_band(gsend.at[2 * t + 1 - core], gcore.at[t], k_send.at[t], k_recv.at[t], core_peer)

        def to_owner(k):
            element = (site + k) % half * 2 + core
            return to_band(gsend.at[element], grecv.at[k], g_send.at[k], g_recv.at[k], element)

        def pair_up(t, carry):
            gsend[2 * t + 1 - core] = source[2 * t + 1 - core].astype(jnp.bfloat16)
            to_core(t).start()
            return carry

        def hand_over(i, carry):
            k = i + 1
            t = (site + k) % half
            to_core(t).wait_recv()
            gsend[2 * t + core] = (source[2 * t + core] + gcore[t].astype(jnp.float32)).astype(jnp.bfloat16)
            to_owner(k).start()
            return carry

        def begin():
            lax.fori_loop(0, half, pair_up, 0)
            lax.fori_loop(0, half - 1, hand_over, 0)

        def end():
            to_core(site).wait_recv()
            total = source[b] + gcore[site].astype(jnp.float32)
            for k in range(1, half):
                to_owner(k).wait_recv()
                total = total + grecv[k].astype(jnp.float32)
            return total

        def drain():
            for t in range(half):
                to_core(t).wait_send()
            for k in range(1, half):
                to_owner(k).wait_send()

        return begin, end, drain

    begin_a, end_a, drain_a = reduction(across, gsend_a, gcore_a, grecv_a, ka_send, ka_recv, ga_send, ga_recv)
    begin_b, end_b, drain_b = reduction(gram, gsend_b, gcore_b, grecv_b, kb_send, kb_recv, gb_send, gb_recv)
    t_across = to_x(total_out, total_in, t_send.at[0], t_recv.at[0])

    filter_chunk(0)
    begin_a()
    pairs(compose)
    own_part()
    filter_chunk(1)
    begin_b()
    total_out[...] = end_a().astype(jnp.bfloat16)
    t_across.start()
    c_across[4].start()
    filter_chunk(2)
    total = end_b()
    c_across[3].wait_recv()
    pairs(far_first)
    t_across.wait_recv()
    total = (total + total_in[...].astype(jnp.float32)) * (1.0 / (2.0 * nbl * nb))

    high = total.astype(jnp.bfloat16)
    low = (total - high.astype(jnp.float32)).astype(jnp.bfloat16)
    basis_copy.wait()
    values = functions[...]
    image_g = jnp.dot(values, high, preferred_element_type=jnp.float32)
    image_g = image_g + jnp.dot(values, low, preferred_element_type=jnp.float32)
    product = image_g * values.astype(jnp.float32)
    top = product.astype(jnp.bfloat16)
    rest = (product - top.astype(jnp.float32)).astype(jnp.bfloat16)
    ones = jnp.ones((16, product.shape[1]), jnp.bfloat16)
    over_last = (((1,), (1,)), ((), ()))
    density = lax.dot_general(ones, top, over_last, preferred_element_type=jnp.float32)
    density = density + lax.dot_general(ones, rest, over_last, preferred_element_type=jnp.float32)
    dens_ref[...] = density[0:1]

    c_across[4].wait_recv()
    pairs(far_last)

    for copy in h_across + [n_across, t_across] + c_across:
        copy.wait_send()
    for when, copy in sent:
        when(copy.wait_send)
    drain_a()
    drain_b()


def finish_kernel(filt_ref, dens_ref, filt_hbm, dens_hbm, sem):
    copies = [
        pltpu.make_async_copy(filt_ref, filt_hbm, sem.at[0]),
        pltpu.make_async_copy(dens_ref, dens_hbm, sem.at[1]),
    ]
    for copy in copies:
        copy.start()
    for copy in copies:
        copy.wait()


def plane_body(nb, coeffs, hamilton, neighbors, basis, occupation):
    elements, nbasis, nbl = coeffs.shape
    points = basis.shape[1]
    n = nbl // 5
    width = neighbors.shape[1]
    half = nb // 2
    dma = pltpu.SemaphoreType.DMA
    hbm = pl.BlockSpec(memory_space=pl.ANY)
    vmem = pl.BlockSpec(memory_space=pltpu.VMEM)
    nz = nb // 4
    forwards = 2 * (4 + 6 * (nz - 1) + 1 + 2 * (nz - 1))
    bf16, f32 = jnp.bfloat16, jnp.float32
    def chunk(rows, columns, dtype=bf16):
        return pltpu.VMEM((elements, rows, columns), dtype)

    rounds = [
        pltpu.VMEM((elements, nbasis, nbasis), bf16),
        pltpu.VMEM((half, nbasis, nbasis), bf16),
        pltpu.VMEM((half, nbasis, nbasis), bf16),
    ]
    operands = [coeffs, hamilton, neighbors.T, occupation.reshape(1, -1), basis]
    operands = [pltpu.with_memory_space_constraint(x, pltpu.HBM) for x in operands]
    filtered, density = pl.pallas_call(
        functools.partial(kernel, nb, n),
        out_shape=(
            jax.ShapeDtypeStruct(coeffs.shape, bf16),
            jax.ShapeDtypeStruct((1, points), f32),
        ),
        in_specs=[hbm] * 5,
        out_specs=(vmem, vmem),
        scratch_shapes=[
            chunk(nbasis, 2 * n), chunk(nbasis, n), chunk(nbasis, n),
            chunk(nbasis // 2, n), chunk(nbasis // 2, n),
            chunk(nbasis, nbl), chunk(nbasis, nbl, f32),
            chunk(nbasis, 2 * n), chunk(nbasis, 2 * n),
            pltpu.VMEM((elements, 6, nbasis, nbasis), bf16),
            pltpu.VMEM((elements, 6, nbasis, nbasis), bf16),
            pltpu.VMEM((width, elements), jnp.int32),
            pltpu.SMEM((width, elements), jnp.int32),
            pltpu.SMEM((width, elements), jnp.int32),
            pltpu.VMEM((1, nbl), jnp.int32),
            pltpu.VMEM((points, nbasis), bf16),
            chunk(nbasis, nbasis, f32), chunk(nbasis, nbasis, f32),
            chunk(nbasis, 5 * nbasis // 2), chunk(nbasis, 5 * nbasis // 2),
            chunk(nbasis, n, f32),
        ] + rounds + rounds + [
            pltpu.VMEM((nbasis, nbasis), bf16),
            pltpu.VMEM((nbasis, nbasis), bf16),
            dma((5,)), dma((5,)),
            dma((3,)), dma((3,)),
            dma((1,)), dma((1,)),
            dma((forwards,)), dma((2 * nb,)),
        ] + [dma((half,))] * 8 + [
            dma((1,)), dma((1,)),
            dma((1,)), dma((2,)), dma((4,)),
            pltpu.SemaphoreType.REGULAR, pltpu.SemaphoreType.REGULAR,
        ],
        compiler_params=pltpu.CompilerParams(
            collective_id=0, has_side_effects=True, vmem_limit_bytes=44 * 2**20),
    )(*operands)
    return pl.pallas_call(
        finish_kernel,
        out_shape=(
            jax.ShapeDtypeStruct(coeffs.shape, bf16),
            jax.ShapeDtypeStruct((1, points), f32),
        ),
        in_specs=[vmem, vmem],
        out_specs=(hbm, hbm),
        scratch_shapes=[dma((2,))],
        compiler_params=pltpu.CompilerParams(vmem_limit_bytes=8 * 2**20),
    )(filtered, density)


def solution(mesh):
    layers, nb = mesh.shape["layer"], mesh.shape["band"]

    def body(coeffs, hamilton, neighbors, basis, occupation):
        elements = coeffs.shape[0]
        one_kernel = (
            layers == 2 and elements == FY * FZ and nb == elements
            and nb % 4 == 0 and nb >= 8 and coeffs.shape[2] % 640 == 0
            and coeffs.shape[1] == 128 and basis.shape[0] == 1
        )
        if one_kernel:
            return plane_body(nb, coeffs, hamilton, neighbors, basis, occupation)
        return general_body(coeffs, hamilton, neighbors, basis, occupation)

    return jax.shard_map(
        body,
        mesh=mesh,
        in_specs=(
            P("layer", None, "band"),
            P("layer", None, None, None),
            P("layer", None),
            P(("layer", "band"), None, None),
            P(),
        ),
        out_specs=(P("layer", None, "band"), P(("layer", "band"), None)),
        check_vma=False,
    )
```

```python
import functools

import jax
import jax.numpy as jnp
from jax import lax
from jax.experimental import pallas as pl
from jax.experimental.pallas import tpu as pltpu
from jax.sharding import PartitionSpec as P

FY = 4
FZ = 4
MESH = pl.DeviceIdType.MESH

center = 0.5
half_width = 1.5


def with_halo(array, sides, width):
    for axis, dim in sides:
        devices, length = (lax.axis_size(axis), array.shape[dim])
        up = [(i, (i + 1) % devices) for i in range(devices - 1)]
        down = [(j, i) for i, j in up]
        last = lax.slice_in_dim(array, length - width, length, axis=dim)
        first = lax.slice_in_dim(array, 0, width, axis=dim)
        before = lax.ppermute(last, axis, up)
        after = lax.ppermute(first, axis, down)
        array = jnp.concatenate([before, array, after], axis=dim)
    return array


def neighbor_product(blocks, nearby):
    return jnp.einsum("ekij,ekjb->eib", blocks, nearby, preferred_element_type=jnp.float32)


def general_body(coeffs, hamilton, neighbors, basis, occupation):
    elements = coeffs.shape[0]
    face_size = FY * FZ
    offset = lax.axis_index("layer") * elements - face_size
    usable = neighbors >= 0
    position = jnp.where(usable, neighbors - offset, 0)
    allowed = usable.astype(jnp.bfloat16)

    def operate(source):
        padded = with_halo(source, (("layer", 0),), face_size)
        inside = source[position[:, :5] - face_size]
        result = neighbor_product(hamilton[:, :5], inside)
        across = padded[position[:, 5:]] * allowed[:, 5:, None, None]
        return result + neighbor_product(hamilton[:, 5:], across)

    start_vals = coeffs.astype(jnp.float32)
    first_image = operate(coeffs)
    filtered_once = ((first_image - center * start_vals) / half_width).astype(jnp.bfloat16)
    second_image = operate(filtered_once)
    filtered = (
        2.0 * (second_image - center * filtered_once.astype(jnp.float32)) / half_width - start_vals
    ).astype(jnp.bfloat16)
    weights = (1 + occupation).astype(jnp.float32) / (2.0 * occupation.shape[0])
    copies = lax.axis_size("band") // elements
    duplicated = jnp.tile(filtered, (copies, 1, 1))
    regrouped = lax.all_to_all(duplicated, "band", split_axis=0, concat_axis=2, tiled=True)
    orbital = jnp.dot(basis[0], regrouped[0], preferred_element_type=jnp.float32)
    density = jnp.sum(orbital * orbital * weights[None, :], axis=1)[None, :]
    return (filtered, density)


def kernel(nb, n, c_hbm, h_hbm, nbr_hbm, occ_hbm, basis_hbm, out_ref, dens_ref, *scratch):
    elements, nbasis, nbl = c_hbm.shape
    cx, cl = scratch[:3], scratch[3:5]
    (cown, ahead, f1o, f1x, hown, hx, nx_v, nown, nx, occ_v, functions, gram, across, row_a, row_b, base,
     gsend_a, gcore_a, grecv_a, gsend_b, gcore_b, grecv_b, total_out, total_in,
     c_send, c_recv, hx_send, hx_recv, n_send, n_recv, f_send, f_recv,
     ka_send, ka_recv, ga_send, ga_recv, kb_send, kb_recv, gb_send, gb_recv, t_send, t_recv,
     lc_sem, lh_sem, misc_sem, x_ready, all_in) = scratch[5:]
    layer, b = lax.axis_index("layer"), lax.axis_index("band")
    other = 1 - layer
    nz = nb // 4
    half = nb // 2
    site = b // 2
    z, y, core = b // 4, (b // 2) % 2, b % 2
    core_peer = b + 1 - 2 * core
    own_cross, x_cross = 6 - layer, 6 - other
    part = nbasis - nbasis // 2
    row_parts = (pl.ds(0, part), pl.ds(part, nbasis - part))
    widths = (2 * n, n, n, n)
    starts = (0, 2 * n, 3 * n, 4 * n)

    def ident(zz, yy, cc):
        return zz * 4 + yy * 2 + cc

    def place(s, side=layer):
        return pl.multiple_of(starts[s] + side * (nbl - widths[s] - 2 * starts[s]), n)

    barrier = pltpu.get_barrier_semaphore()

    @pl.when(layer == 0)
    def _():
        pl.semaphore_signal(barrier, inc=1, device_id={"layer": other, "band": b}, device_id_type=MESH)

    @pl.when(layer == 1)
    def _():
        pl.semaphore_wait(barrier, 1)
        pl.semaphore_signal(x_ready, inc=1, device_id={"layer": other, "band": b}, device_id_type=MESH)

    @pl.when(layer == 0)
    def _():
        pl.semaphore_wait(x_ready, 1)

    def to_x(src, dst, send, recv):
        return pltpu.make_async_remote_copy(
            src_ref=src, dst_ref=dst, send_sem=send, recv_sem=recv,
            device_id={"layer": other, "band": b}, device_id_type=MESH)

    def to_band(src, dst, send, recv, peer):
        return pltpu.make_async_remote_copy(
            src_ref=src, dst_ref=dst, send_sem=send, recv_sem=recv,
            device_id={"layer": layer, "band": peer}, device_id_type=MESH)

    pieces = ((0, 3), (3, 3))
    h_across = [
        to_x(h_hbm.at[b, pl.ds(0, 3)], hx.at[b, pl.ds(0, 3)], hx_send.at[0], hx_recv.at[0]),
        to_x(h_hbm.at[b, pl.ds(3, 2)], hx.at[b, pl.ds(3, 2)], hx_send.at[1], hx_recv.at[1]),
        to_x(h_hbm.at[b, pl.ds(own_cross, 1)], hx.at[b, pl.ds(5, 1)], hx_send.at[2], hx_recv.at[2]),
    ]
    n_across = to_x(nbr_hbm, nx_v, n_send.at[0], n_recv.at[0])
    c_across = [
        to_x(c_hbm.at[:, :, pl.ds(place(s, other), widths[s])], cx[s], c_send.at[s], c_recv.at[s]) for s in range(3)
    ] + [
        to_x(c_hbm.at[:, row_parts[i], pl.ds(place(3, other), n)], cl[i], c_send.at[3 + i], c_recv.at[3 + i])
        for i in range(2)
    ]
    for copy in h_across + [n_across] + c_across[:4]:
        copy.start()

    n_copy = pltpu.make_async_copy(nbr_hbm, nown, misc_sem.at[0])
    occ_copy = pltpu.make_async_copy(occ_hbm.at[:, pl.ds(pl.multiple_of(b * nbl, n), nbl)], occ_v, misc_sem.at[2])
    basis_copy = pltpu.make_async_copy(basis_hbm.at[0], functions, misc_sem.at[3])
    h_copies = [
        pltpu.make_async_copy(h_hbm.at[:, pl.ds(0, 5)], hown.at[:, pl.ds(0, 5)], lh_sem.at[0]),
        pltpu.make_async_copy(h_hbm.at[:, pl.ds(own_cross, 1)], hown.at[:, pl.ds(5, 1)], lh_sem.at[1]),
    ]
    c_copy = pltpu.make_async_copy(c_hbm, cown, lc_sem.at[0])
    for copy in [n_copy, occ_copy, c_copy] + h_copies + [basis_copy]:
        copy.start()

    @pl.when(layer == 0)
    def _():
        for peer in [core_peer] + [(site + k) % half * 2 + core for k in range(1, half)]:
            pl.semaphore_signal(barrier, inc=1, device_id={"layer": layer, "band": peer}, device_id_type=MESH)
        pl.semaphore_wait(barrier, half)
        pl.semaphore_signal(all_in, inc=1, device_id={"layer": other, "band": b}, device_id_type=MESH)

    @pl.when(layer == 1)
    def _():
        pl.semaphore_wait(all_in, 1)

    def groups(body, size, low=0, high=elements):
        def several(t, carry):
            body([size * t + i for i in range(size)])
            return carry
        lax.fori_loop(low // size, high // size, several, 0)

    def pairs(body):
        groups(body, 2)

    for copy in [n_copy, c_copy] + h_copies:
        copy.wait()

    def in_plane(at):
        def one(e):
            row = jnp.concatenate([hown[e, k] for k in range(5)], axis=1)
            parts = jnp.concatenate([cown[lax.rem(nown[k, e], elements)] for k in range(5)], axis=0)
            return jnp.dot(row, parts, preferred_element_type=jnp.float32) - center * cown[e].astype(jnp.float32)
        for e, value in zip(at, [one(e) for e in at]):
            ahead[e] = value

    sent = []

    def always(body):
        body()

    def forward(block, i, peer, when=always):
        slot = len(sent)
        at, size = pieces[i]
        held = hx.at[block, pl.ds(at, size)]
        copy = to_band(held, held, f_send.at[slot], f_recv.at[block * 2 + i], peer)
        sent.append((when, copy))
        when(copy.start)

    def arrived(block, i, peer):
        at, size = pieces[i]
        held = hx.at[block, pl.ds(at, size)]
        to_band(held, held, f_send.at[0], f_recv.at[block * 2 + i], peer).wait_recv()

    def inside(zz):
        return pl.when(jnp.logical_and(zz >= 0, zz < nz))

    def both_inside(za, zb):
        return pl.when(jnp.logical_and(jnp.minimum(za, zb) >= 0, jnp.maximum(za, zb) < nz))

    y_peer = ident(z, 1 - y, core)
    groups(in_plane, 2, 0, 8)
    for i in range(2):
        h_across[i].wait_recv()
        if i == 1:
            h_across[2].wait_recv()
        for step in (1, -1):
            forward(b, i, ident(z + step, y, core), inside(z + step))
        forward(b, i, y_peer)
        forward(b, i, core_peer)
    groups(in_plane, 2, 8, elements)

    def over_y(away):
        for i in range(2):
            for step in (1, -1) if away else (1,):
                from_z = z - step * away
                block = ident(from_z, 1 - y, core)
                if away:
                    inside(from_z)(functools.partial(arrived, block, i, y_peer))
                    forward(block, i, core_peer, inside(from_z))
                else:
                    arrived(block, i, y_peer)
                    forward(block, i, core_peer)

    for away in range(1, nz):
        for i in range(2):
            for step in (1, -1):
                from_z = z - step * away
                block = ident(from_z, y, core)
                inside(from_z)(functools.partial(arrived, block, i, ident(z - step, y, core)))
                forward(block, i, ident(z + step, y, core), both_inside(from_z, z + step))
                forward(block, i, y_peer, inside(from_z))
                forward(block, i, core_peer, inside(from_z))
        over_y(away - 1)
    over_y(nz - 1)
    for zz in range(nz):
        for yy in range(2):
            for i in range(2):
                arrived(ident(zz, yy, 1 - core), i, core_peer)

    n_across.wait_recv()
    nx_copy = pltpu.make_async_copy(nx_v, nx, misc_sem.at[1])
    nx_copy.start()
    for copy in [nx_copy, occ_copy]:
        copy.wait()

    def image(blocks, table, e, cross, near, far):
        row = jnp.concatenate([blocks[e, k] for k in range(6)], axis=1)
        parts = [near(lax.rem(table[k, e], elements)) for k in range(5)]
        parts.append(far(lax.rem(table[cross, e], elements)))
        return jnp.dot(row, jnp.concatenate(parts, axis=0), preferred_element_type=jnp.float32)

    def once(got):
        return (got * (1.0 / half_width)).astype(jnp.bfloat16)

    def twice(got, middle, start):
        return (got - center * middle.astype(jnp.float32)) * (2.0 / half_width) - start.astype(jnp.float32)

    def square(value, weight):
        scaled = (value.astype(jnp.float32) * weight).astype(jnp.bfloat16)
        return lax.dot_general(scaled, value, (((1,), (1,)), ((), ())), preferred_element_type=jnp.float32)

    def filter_chunk(s):
        c_across[s].wait_recv()
        width = widths[s]
        columns = pl.ds(place(s), width)
        lanes = pl.ds(0, width)
        weight = (1 + occ_v[:, columns]).astype(jnp.float32)

        def own(e):
            return cown[e, :, columns]

        def far(e):
            return cx[s][e]

        def mine(e):
            return f1o[e, :, lanes]

        def theirs(e):
            return f1x[e, :, lanes]

        def first(at):
            across_x = [jnp.dot(hown[e, 5], far(lax.rem(nown[own_cross, e], elements)), preferred_element_type=jnp.float32)
                        for e in at]
            left = [once(ahead[e, :, columns] + got) for e, got in zip(at, across_x)]
            right = [once(image(hx, nx, e, x_cross, far, own) - center * far(e).astype(jnp.float32)) for e in at]
            for e, p, q in zip(at, left, right):
                f1o[e, :, lanes] = p
                f1x[e, :, lanes] = q

        def second(at):
            got = [twice(image(hown, nown, e, own_cross, mine, theirs), mine(e), own(e)).astype(jnp.bfloat16) for e in at]
            if s < 2:
                sums = [square(value, weight) for value in got]
                if s > 0:
                    sums = [added + gram[e] for e, added in zip(at, sums)]
                for e, added in zip(at, sums):
                    gram[e] = added
            for e, value in zip(at, got):
                out_ref[e, :, columns] = value

        def second_x(at):
            got = [twice(image(hx, nx, e, x_cross, theirs, mine), theirs(e), far(e)).astype(jnp.bfloat16) for e in at]
            for e, added in zip(at, [square(value, weight) for value in got]):
                across[e] = added

        size = 4
        groups(first, size)
        if s == 0:
            groups(second_x, size)
        groups(second, size)

    last_columns = pl.ds(place(3), n)

    def compose(at):
        def one(e, k):
            there = lax.rem(nown[own_cross, e], elements)
            beside = lax.rem(nown[k, e], elements)
            if k == 0:
                which = 0
            else:
                target = lax.rem(nown[own_cross, beside], elements)
                which = 0
                for j in range(1, 5):
                    which = jnp.where(lax.rem(nx[j, there], elements) == target, j, which)
            row = jnp.concatenate([hown[e, k], hown[e, 5]], axis=1)
            parts = jnp.concatenate([hown[beside, 5], hx[there, which]], axis=0)
            got = jnp.dot(row, parts, preferred_element_type=jnp.float32)
            if k == 0:
                got = got - (2.0 * center) * hown[e, 5].astype(jnp.float32)
            return (got * (2.0 / half_width / half_width)).astype(jnp.bfloat16)
        rows = [[one(e, k) for k in range(5)] for e in at]
        for e, row in zip(at, rows):
            row_a[e] = jnp.concatenate([block[:, :part] for block in row], axis=1)
            row_b[e] = jnp.concatenate([block[:, part:] for block in row], axis=1)

    def own_part():
        def own(e):
            return cown[e, :, last_columns]

        def mine(e):
            return f1o[e, :, pl.ds(0, n)]

        def theirs(e):
            return f1x[e, :, pl.ds(0, n)]

        def first(at):
            left = [once(ahead[e, :, last_columns]) for e in at]
            right = [once(jnp.dot(hx[e, 5], own(lax.rem(nx[x_cross, e], elements)), preferred_element_type=jnp.float32))
                     for e in at]
            for e, p, q in zip(at, left, right):
                f1o[e, :, pl.ds(0, n)] = p
                f1x[e, :, pl.ds(0, n)] = q

        def second(at):
            got = [twice(image(hown, nown, e, own_cross, mine, theirs), mine(e), own(e)) for e in at]
            for e, value in zip(at, got):
                base[e] = value

        groups(first, 4)
        groups(second, 4)

    def far_part(row, held, e):
        parts = [held[lax.rem(nown[own_cross, lax.rem(nown[k, e], elements)], elements)] for k in range(5)]
        return base[e] + jnp.dot(row[e], jnp.concatenate(parts, axis=0), preferred_element_type=jnp.float32)

    def far_first(at):
        for e, value in zip(at, [far_part(row_a, cl[0], e) for e in at]):
            base[e] = value

    def far_last(at):
        for e, value in zip(at, [far_part(row_b, cl[1], e) for e in at]):
            out_ref[e, :, last_columns] = value.astype(jnp.bfloat16)

    def reduction(source, gsend, gcore, grecv, k_send, k_recv, g_send, g_recv):
        def to_core(t):
            return to_band(gsend.at[2 * t + 1 - core], gcore.at[t], k_send.at[t], k_recv.at[t], core_peer)

        def to_owner(k):
            element = (site + k) % half * 2 + core
            return to_band(gsend.at[element], grecv.at[k], g_send.at[k], g_recv.at[k], element)

        def pair_up(t, carry):
            gsend[2 * t + 1 - core] = source[2 * t + 1 - core].astype(jnp.bfloat16)
            to_core(t).start()
            return carry

        def hand_over(i, carry):
            k = i + 1
            t = (site + k) % half
            to_core(t).wait_recv()
            gsend[2 * t + core] = (source[2 * t + core] + gcore[t].astype(jnp.float32)).astype(jnp.bfloat16)
            to_owner(k).start()
            return carry

        def begin():
            lax.fori_loop(0, half, pair_up, 0)

        def pass_on():
            lax.fori_loop(0, half - 1, hand_over, 0)

        def end():
            to_core(site).wait_recv()
            total = source[b] + gcore[site].astype(jnp.float32)
            for k in range(1, half):
                to_owner(k).wait_recv()
                total = total + grecv[k].astype(jnp.float32)
            return total

        def drain():
            for t in range(half):
                to_core(t).wait_send()
            for k in range(1, half):
                to_owner(k).wait_send()

        return begin, pass_on, end, drain

    begin_a, pass_a, end_a, drain_a = reduction(across, gsend_a, gcore_a, grecv_a, ka_send, ka_recv, ga_send, ga_recv)
    begin_b, pass_b, end_b, drain_b = reduction(gram, gsend_b, gcore_b, grecv_b, kb_send, kb_recv, gb_send, gb_recv)
    t_across = to_x(total_out, total_in, t_send.at[0], t_recv.at[0])

    filter_chunk(0)
    begin_a()
    pairs(compose)
    pass_a()
    own_part()
    filter_chunk(1)
    begin_b()
    total_out[...] = end_a().astype(jnp.bfloat16)
    t_across.start()
    c_across[4].start()
    pass_b()
    filter_chunk(2)
    total = end_b()
    c_across[3].wait_recv()
    groups(far_first, 4)
    t_across.wait_recv()
    total = (total + total_in[...].astype(jnp.float32)) * (1.0 / (2.0 * nbl * nb))

    high = total.astype(jnp.bfloat16)
    low = (total - high.astype(jnp.float32)).astype(jnp.bfloat16)
    basis_copy.wait()
    values = functions[...]
    image_g = jnp.dot(values, high, preferred_element_type=jnp.float32)
    image_g = image_g + jnp.dot(values, low, preferred_element_type=jnp.float32)
    product = image_g * values.astype(jnp.float32)
    top = product.astype(jnp.bfloat16)
    rest = (product - top.astype(jnp.float32)).astype(jnp.bfloat16)
    ones = jnp.ones((16, product.shape[1]), jnp.bfloat16)
    over_last = (((1,), (1,)), ((), ()))
    density = lax.dot_general(ones, top, over_last, preferred_element_type=jnp.float32)
    density = density + lax.dot_general(ones, rest, over_last, preferred_element_type=jnp.float32)
    dens_ref[...] = density[0:1]

    c_across[4].wait_recv()
    groups(far_last, 4)

    for copy in h_across + [n_across, t_across] + c_across:
        copy.wait_send()
    for when, copy in sent:
        when(copy.wait_send)
    drain_a()
    drain_b()


def finish_kernel(filt_ref, dens_ref, filt_hbm, dens_hbm, sem):
    copies = [
        pltpu.make_async_copy(filt_ref, filt_hbm, sem.at[0]),
        pltpu.make_async_copy(dens_ref, dens_hbm, sem.at[1]),
    ]
    for copy in copies:
        copy.start()
    for copy in copies:
        copy.wait()


def plane_body(nb, coeffs, hamilton, neighbors, basis, occupation):
    elements, nbasis, nbl = coeffs.shape
    points = basis.shape[1]
    n = nbl // 5
    width = neighbors.shape[1]
    half = nb // 2
    dma = pltpu.SemaphoreType.DMA
    hbm = pl.BlockSpec(memory_space=pl.ANY)
    vmem = pl.BlockSpec(memory_space=pltpu.VMEM)
    nz = nb // 4
    forwards = 2 * (4 + 6 * (nz - 1) + 1 + 2 * (nz - 1))
    bf16, f32 = jnp.bfloat16, jnp.float32
    def chunk(rows, columns, dtype=bf16):
        return pltpu.VMEM((elements, rows, columns), dtype)

    rounds = [
        pltpu.VMEM((elements, nbasis, nbasis), bf16),
        pltpu.VMEM((half, nbasis, nbasis), bf16),
        pltpu.VMEM((half, nbasis, nbasis), bf16),
    ]
    operands = [coeffs, hamilton, neighbors.T, occupation.reshape(1, -1), basis]
    operands = [pltpu.with_memory_space_constraint(x, pltpu.HBM) for x in operands]
    filtered, density = pl.pallas_call(
        functools.partial(kernel, nb, n),
        out_shape=(
            jax.ShapeDtypeStruct(coeffs.shape, bf16),
            jax.ShapeDtypeStruct((1, points), f32),
        ),
        in_specs=[hbm] * 5,
        out_specs=(vmem, vmem),
        scratch_shapes=[
            chunk(nbasis, 2 * n), chunk(nbasis, n), chunk(nbasis, n),
            chunk(nbasis - nbasis // 2, n), chunk(nbasis // 2, n),
            chunk(nbasis, nbl), chunk(nbasis, nbl, f32),
            chunk(nbasis, 2 * n), chunk(nbasis, 2 * n),
            pltpu.VMEM((elements, 6, nbasis, nbasis), bf16),
            pltpu.VMEM((elements, 6, nbasis, nbasis), bf16),
            pltpu.VMEM((width, elements), jnp.int32),
            pltpu.SMEM((width, elements), jnp.int32),
            pltpu.SMEM((width, elements), jnp.int32),
            pltpu.VMEM((1, nbl), jnp.int32),
            pltpu.VMEM((points, nbasis), bf16),
            chunk(nbasis, nbasis, f32), chunk(nbasis, nbasis, f32),
            chunk(nbasis, 5 * (nbasis - nbasis // 2)), chunk(nbasis, 5 * (nbasis // 2)),
            chunk(nbasis, n, f32),
        ] + rounds + rounds + [
            pltpu.VMEM((nbasis, nbasis), bf16),
            pltpu.VMEM((nbasis, nbasis), bf16),
            dma((5,)), dma((5,)),
            dma((3,)), dma((3,)),
            dma((1,)), dma((1,)),
            dma((forwards,)), dma((2 * nb,)),
        ] + [dma((half,))] * 8 + [
            dma((1,)), dma((1,)),
            dma((1,)), dma((2,)), dma((4,)),
            pltpu.SemaphoreType.REGULAR, pltpu.SemaphoreType.REGULAR,
        ],
        compiler_params=pltpu.CompilerParams(
            collective_id=0, has_side_effects=True, vmem_limit_bytes=44 * 2**20),
    )(*operands)
    return pl.pallas_call(
        finish_kernel,
        out_shape=(
            jax.ShapeDtypeStruct(coeffs.shape, bf16),
            jax.ShapeDtypeStruct((1, points), f32),
        ),
        in_specs=[vmem, vmem],
        out_specs=(hbm, hbm),
        scratch_shapes=[dma((2,))],
        compiler_params=pltpu.CompilerParams(vmem_limit_bytes=8 * 2**20),
    )(filtered, density)


def solution(mesh):
    layers, nb = mesh.shape["layer"], mesh.shape["band"]

    def body(coeffs, hamilton, neighbors, basis, occupation):
        elements = coeffs.shape[0]
        one_kernel = (
            layers == 2 and elements == FY * FZ and nb == elements
            and nb % 4 == 0 and nb >= 8 and coeffs.shape[2] % 640 == 0
            and coeffs.shape[1] == 128 and basis.shape[0] == 1
        )
        if one_kernel:
            return plane_body(nb, coeffs, hamilton, neighbors, basis, occupation)
        return general_body(coeffs, hamilton, neighbors, basis, occupation)

    return jax.shard_map(
        body,
        mesh=mesh,
        in_specs=(
            P("layer", None, "band"),
            P("layer", None, None, None),
            P("layer", None),
            P(("layer", "band"), None, None),
            P(),
        ),
        out_specs=(P("layer", None, "band"), P(("layer", "band"), None)),
        check_vma=False,
    )
```

```python
import functools

import jax
import jax.numpy as jnp
from jax import lax
from jax.experimental import pallas as pl
from jax.experimental.pallas import tpu as pltpu
from jax.sharding import PartitionSpec as P

FY = 4
FZ = 4
MESH = pl.DeviceIdType.MESH

center = 0.5
half_width = 1.5


def with_halo(array, sides, width):
    for axis, dim in sides:
        devices, length = (lax.axis_size(axis), array.shape[dim])
        up = [(i, (i + 1) % devices) for i in range(devices - 1)]
        down = [(j, i) for i, j in up]
        last = lax.slice_in_dim(array, length - width, length, axis=dim)
        first = lax.slice_in_dim(array, 0, width, axis=dim)
        before = lax.ppermute(last, axis, up)
        after = lax.ppermute(first, axis, down)
        array = jnp.concatenate([before, array, after], axis=dim)
    return array


def neighbor_product(blocks, nearby):
    return jnp.einsum("ekij,ekjb->eib", blocks, nearby, preferred_element_type=jnp.float32)


def general_body(coeffs, hamilton, neighbors, basis, occupation):
    elements = coeffs.shape[0]
    face_size = FY * FZ
    offset = lax.axis_index("layer") * elements - face_size
    usable = neighbors >= 0
    position = jnp.where(usable, neighbors - offset, 0)
    allowed = usable.astype(jnp.bfloat16)

    def operate(source):
        padded = with_halo(source, (("layer", 0),), face_size)
        inside = source[position[:, :5] - face_size]
        result = neighbor_product(hamilton[:, :5], inside)
        across = padded[position[:, 5:]] * allowed[:, 5:, None, None]
        return result + neighbor_product(hamilton[:, 5:], across)

    start_vals = coeffs.astype(jnp.float32)
    first_image = operate(coeffs)
    filtered_once = ((first_image - center * start_vals) / half_width).astype(jnp.bfloat16)
    second_image = operate(filtered_once)
    filtered = (
        2.0 * (second_image - center * filtered_once.astype(jnp.float32)) / half_width - start_vals
    ).astype(jnp.bfloat16)
    weights = (1 + occupation).astype(jnp.float32) / (2.0 * occupation.shape[0])
    copies = lax.axis_size("band") // elements
    duplicated = jnp.tile(filtered, (copies, 1, 1))
    regrouped = lax.all_to_all(duplicated, "band", split_axis=0, concat_axis=2, tiled=True)
    orbital = jnp.dot(basis[0], regrouped[0], preferred_element_type=jnp.float32)
    density = jnp.sum(orbital * orbital * weights[None, :], axis=1)[None, :]
    return (filtered, density)


def kernel(nb, n, c_hbm, h_hbm, nbr_hbm, occ_hbm, basis_hbm, out_ref, dens_ref, *scratch):
    elements, nbasis, nbl = c_hbm.shape
    cx, cl = scratch[:3], scratch[3:5]
    (cown, ahead, f1o, f1x, hown, hx, nx_v, nown, nx, occ_v, functions, gram, across, row_a, row_b, base,
     gsend_a, gcore_a, grecv_a, gsend_b, gcore_b, grecv_b, total_out, total_in,
     c_send, c_recv, hx_send, hx_recv, n_send, n_recv, f_send, f_recv,
     ka_send, ka_recv, ga_send, ga_recv, kb_send, kb_recv, gb_send, gb_recv, t_send, t_recv,
     lc_sem, lh_sem, misc_sem, x_ready, all_in) = scratch[5:]
    layer, b = lax.axis_index("layer"), lax.axis_index("band")
    other = 1 - layer
    nz = nb // 4
    half = nb // 2
    site = b // 2
    z, y, core = b // 4, (b // 2) % 2, b % 2
    core_peer = b + 1 - 2 * core
    own_cross, x_cross = 6 - layer, 6 - other
    part = nbasis - nbasis // 4
    row_parts = (pl.ds(0, part), pl.ds(part, nbasis - part))
    widths = (2 * n, n, n, n)
    starts = (0, 2 * n, 3 * n, 4 * n)

    def ident(zz, yy, cc):
        return zz * 4 + yy * 2 + cc

    def place(s, side=layer):
        return pl.multiple_of(starts[s] + side * (nbl - widths[s] - 2 * starts[s]), n)

    barrier = pltpu.get_barrier_semaphore()

    @pl.when(layer == 0)
    def _():
        pl.semaphore_signal(barrier, inc=1, device_id={"layer": other, "band": b}, device_id_type=MESH)

    @pl.when(layer == 1)
    def _():
        pl.semaphore_wait(barrier, 1)
        pl.semaphore_signal(x_ready, inc=1, device_id={"layer": other, "band": b}, device_id_type=MESH)

    @pl.when(layer == 0)
    def _():
        pl.semaphore_wait(x_ready, 1)

    def to_x(src, dst, send, recv):
        return pltpu.make_async_remote_copy(
            src_ref=src, dst_ref=dst, send_sem=send, recv_sem=recv,
            device_id={"layer": other, "band": b}, device_id_type=MESH)

    def to_band(src, dst, send, recv, peer):
        return pltpu.make_async_remote_copy(
            src_ref=src, dst_ref=dst, send_sem=send, recv_sem=recv,
            device_id={"layer": layer, "band": peer}, device_id_type=MESH)

    pieces = ((0, 3), (3, 3))
    h_across = [
        to_x(h_hbm.at[b, pl.ds(0, 3)], hx.at[b, pl.ds(0, 3)], hx_send.at[0], hx_recv.at[0]),
        to_x(h_hbm.at[b, pl.ds(3, 2)], hx.at[b, pl.ds(3, 2)], hx_send.at[1], hx_recv.at[1]),
        to_x(h_hbm.at[b, pl.ds(own_cross, 1)], hx.at[b, pl.ds(5, 1)], hx_send.at[2], hx_recv.at[2]),
    ]
    n_across = to_x(nbr_hbm, nx_v, n_send.at[0], n_recv.at[0])
    c_across = [
        to_x(c_hbm.at[:, :, pl.ds(place(s, other), widths[s])], cx[s], c_send.at[s], c_recv.at[s]) for s in range(3)
    ] + [
        to_x(c_hbm.at[:, row_parts[i], pl.ds(place(3, other), n)], cl[i], c_send.at[3 + i], c_recv.at[3 + i])
        for i in range(2)
    ]
    for copy in h_across + [n_across] + c_across[:3]:
        copy.start()

    n_copy = pltpu.make_async_copy(nbr_hbm, nown, misc_sem.at[0])
    occ_copy = pltpu.make_async_copy(occ_hbm.at[:, pl.ds(pl.multiple_of(b * nbl, n), nbl)], occ_v, misc_sem.at[2])
    basis_copy = pltpu.make_async_copy(basis_hbm.at[0], functions, misc_sem.at[3])
    h_copies = [
        pltpu.make_async_copy(h_hbm.at[:, pl.ds(0, 5)], hown.at[:, pl.ds(0, 5)], lh_sem.at[0]),
        pltpu.make_async_copy(h_hbm.at[:, pl.ds(own_cross, 1)], hown.at[:, pl.ds(5, 1)], lh_sem.at[1]),
    ]
    c_copy = pltpu.make_async_copy(c_hbm, cown, lc_sem.at[0])
    for copy in [n_copy, occ_copy, c_copy] + h_copies + [basis_copy]:
        copy.start()

    @pl.when(layer == 0)
    def _():
        for peer in [core_peer] + [(site + k) % half * 2 + core for k in range(1, half)]:
            pl.semaphore_signal(barrier, inc=1, device_id={"layer": layer, "band": peer}, device_id_type=MESH)
        pl.semaphore_wait(barrier, half)
        pl.semaphore_signal(all_in, inc=1, device_id={"layer": other, "band": b}, device_id_type=MESH)

    @pl.when(layer == 1)
    def _():
        pl.semaphore_wait(all_in, 1)

    def groups(body, size, low=0, high=elements):
        def several(t, carry):
            body([size * t + i for i in range(size)])
            return carry
        lax.fori_loop(low // size, high // size, several, 0)

    def pairs(body):
        groups(body, 2)

    for copy in [n_copy, c_copy] + h_copies:
        copy.wait()

    def in_plane(at):
        def one(e):
            row = jnp.concatenate([hown[e, k] for k in range(5)], axis=1)
            parts = jnp.concatenate([cown[lax.rem(nown[k, e], elements)] for k in range(5)], axis=0)
            return jnp.dot(row, parts, preferred_element_type=jnp.float32) - center * cown[e].astype(jnp.float32)
        for e, value in zip(at, [one(e) for e in at]):
            ahead[e] = value

    sent = []

    def always(body):
        body()

    def forward(block, i, peer, when=always):
        slot = len(sent)
        at, size = pieces[i]
        held = hx.at[block, pl.ds(at, size)]
        copy = to_band(held, held, f_send.at[slot], f_recv.at[block * 2 + i], peer)
        sent.append((when, copy))
        when(copy.start)

    def arrived(block, i, peer):
        at, size = pieces[i]
        held = hx.at[block, pl.ds(at, size)]
        to_band(held, held, f_send.at[0], f_recv.at[block * 2 + i], peer).wait_recv()

    def inside(zz):
        return pl.when(jnp.logical_and(zz >= 0, zz < nz))

    def both_inside(za, zb):
        return pl.when(jnp.logical_and(jnp.minimum(za, zb) >= 0, jnp.maximum(za, zb) < nz))

    y_peer = ident(z, 1 - y, core)
    groups(in_plane, 2, 0, 8)
    for i in range(2):
        h_across[i].wait_recv()
        if i == 1:
            h_across[2].wait_recv()
        for step in (1, -1):
            forward(b, i, ident(z + step, y, core), inside(z + step))
        forward(b, i, y_peer)
        forward(b, i, core_peer)
    groups(in_plane, 2, 8, elements)

    def over_y(away):
        for i in range(2):
            for step in (1, -1) if away else (1,):
                from_z = z - step * away
                block = ident(from_z, 1 - y, core)
                if away:
                    inside(from_z)(functools.partial(arrived, block, i, y_peer))
                    forward(block, i, core_peer, inside(from_z))
                else:
                    arrived(block, i, y_peer)
                    forward(block, i, core_peer)

    for away in range(1, nz):
        for i in range(2):
            for step in (1, -1):
                from_z = z - step * away
                block = ident(from_z, y, core)
                inside(from_z)(functools.partial(arrived, block, i, ident(z - step, y, core)))
                forward(block, i, ident(z + step, y, core), both_inside(from_z, z + step))
                forward(block, i, y_peer, inside(from_z))
                forward(block, i, core_peer, inside(from_z))
        over_y(away - 1)
    over_y(nz - 1)
    for zz in range(nz):
        for yy in range(2):
            for i in range(2):
                arrived(ident(zz, yy, 1 - core), i, core_peer)

    n_across.wait_recv()
    nx_copy = pltpu.make_async_copy(nx_v, nx, misc_sem.at[1])
    nx_copy.start()
    for copy in [nx_copy, occ_copy]:
        copy.wait()

    def image(blocks, table, e, cross, near, far):
        row = jnp.concatenate([blocks[e, k] for k in range(6)], axis=1)
        parts = [near(lax.rem(table[k, e], elements)) for k in range(5)]
        parts.append(far(lax.rem(table[cross, e], elements)))
        return jnp.dot(row, jnp.concatenate(parts, axis=0), preferred_element_type=jnp.float32)

    def once(got):
        return (got * (1.0 / half_width)).astype(jnp.bfloat16)

    def twice(got, middle, start):
        return (got - center * middle.astype(jnp.float32)) * (2.0 / half_width) - start.astype(jnp.float32)

    def square(value, weight):
        scaled = (value.astype(jnp.float32) * weight).astype(jnp.bfloat16)
        return lax.dot_general(scaled, value, (((1,), (1,)), ((), ())), preferred_element_type=jnp.float32)

    def filter_chunk(s):
        c_across[s].wait_recv()
        width = widths[s]
        columns = pl.ds(place(s), width)
        lanes = pl.ds(0, width)
        weight = (1 + occ_v[:, columns]).astype(jnp.float32)

        def own(e):
            return cown[e, :, columns]

        def far(e):
            return cx[s][e]

        def mine(e):
            return f1o[e, :, lanes]

        def theirs(e):
            return f1x[e, :, lanes]

        def first(at):
            across_x = [jnp.dot(hown[e, 5], far(lax.rem(nown[own_cross, e], elements)), preferred_element_type=jnp.float32)
                        for e in at]
            left = [once(ahead[e, :, columns] + got) for e, got in zip(at, across_x)]
            right = [once(image(hx, nx, e, x_cross, far, own) - center * far(e).astype(jnp.float32)) for e in at]
            for e, p, q in zip(at, left, right):
                f1o[e, :, lanes] = p
                f1x[e, :, lanes] = q

        def second(at):
            got = [twice(image(hown, nown, e, own_cross, mine, theirs), mine(e), own(e)).astype(jnp.bfloat16) for e in at]
            if s < 2:
                sums = [square(value, weight) for value in got]
                if s > 0:
                    sums = [added + gram[e] for e, added in zip(at, sums)]
                for e, added in zip(at, sums):
                    gram[e] = added
            for e, value in zip(at, got):
                out_ref[e, :, columns] = value

        def second_x(at):
            got = [twice(image(hx, nx, e, x_cross, theirs, mine), theirs(e), far(e)).astype(jnp.bfloat16) for e in at]
            for e, added in zip(at, [square(value, weight) for value in got]):
                across[e] = added

        size = 4
        groups(first, size)
        if s == 0:
            groups(second_x, size)
        groups(second, size)

    last_columns = pl.ds(place(3), n)

    def compose(at):
        def one(e, k):
            there = lax.rem(nown[own_cross, e], elements)
            beside = lax.rem(nown[k, e], elements)
            if k == 0:
                which = 0
            else:
                target = lax.rem(nown[own_cross, beside], elements)
                which = 0
                for j in range(1, 5):
                    which = jnp.where(lax.rem(nx[j, there], elements) == target, j, which)
            row = jnp.concatenate([hown[e, k], hown[e, 5]], axis=1)
            parts = jnp.concatenate([hown[beside, 5], hx[there, which]], axis=0)
            got = jnp.dot(row, parts, preferred_element_type=jnp.float32)
            if k == 0:
                got = got - (2.0 * center) * hown[e, 5].astype(jnp.float32)
            return (got * (2.0 / half_width / half_width)).astype(jnp.bfloat16)
        rows = [[one(e, k) for k in range(5)] for e in at]
        for e, row in zip(at, rows):
            row_a[e] = jnp.concatenate([block[:, :part] for block in row], axis=1)
            row_b[e] = jnp.concatenate([block[:, part:] for block in row], axis=1)

    def own_part():
        def own(e):
            return cown[e, :, last_columns]

        def mine(e):
            return f1o[e, :, pl.ds(0, n)]

        def theirs(e):
            return f1x[e, :, pl.ds(0, n)]

        def first(at):
            left = [once(ahead[e, :, last_columns]) for e in at]
            right = [once(jnp.dot(hx[e, 5], own(lax.rem(nx[x_cross, e], elements)), preferred_element_type=jnp.float32))
                     for e in at]
            for e, p, q in zip(at, left, right):
                f1o[e, :, pl.ds(0, n)] = p
                f1x[e, :, pl.ds(0, n)] = q

        def second(at):
            got = [twice(image(hown, nown, e, own_cross, mine, theirs), mine(e), own(e)) for e in at]
            for e, value in zip(at, got):
                base[e] = value

        groups(first, 4)
        groups(second, 4)

    def far_part(row, held, e):
        parts = [held[lax.rem(nown[own_cross, lax.rem(nown[k, e], elements)], elements)] for k in range(5)]
        return base[e] + jnp.dot(row[e], jnp.concatenate(parts, axis=0), preferred_element_type=jnp.float32)

    def far_first(at):
        for e, value in zip(at, [far_part(row_a, cl[0], e) for e in at]):
            base[e] = value

    def far_last(at):
        for e, value in zip(at, [far_part(row_b, cl[1], e) for e in at]):
            out_ref[e, :, last_columns] = value.astype(jnp.bfloat16)

    def reduction(source, gsend, gcore, grecv, k_send, k_recv, g_send, g_recv):
        def to_core(t):
            return to_band(gsend.at[2 * t + 1 - core], gcore.at[t], k_send.at[t], k_recv.at[t], core_peer)

        def to_owner(k):
            element = (site + k) % half * 2 + core
            return to_band(gsend.at[element], grecv.at[k], g_send.at[k], g_recv.at[k], element)

        def pair_up(t, carry):
            gsend[2 * t + 1 - core] = source[2 * t + 1 - core].astype(jnp.bfloat16)
            to_core(t).start()
            return carry

        def hand_over(i, carry):
            k = i + 1
            t = (site + k) % half
            to_core(t).wait_recv()
            gsend[2 * t + core] = (source[2 * t + core] + gcore[t].astype(jnp.float32)).astype(jnp.bfloat16)
            to_owner(k).start()
            return carry

        def begin():
            lax.fori_loop(0, half, pair_up, 0)

        def pass_on():
            lax.fori_loop(0, half - 1, hand_over, 0)

        def end():
            to_core(site).wait_recv()
            total = source[b] + gcore[site].astype(jnp.float32)
            for k in range(1, half):
                to_owner(k).wait_recv()
                total = total + grecv[k].astype(jnp.float32)
            return total

        def drain():
            for t in range(half):
                to_core(t).wait_send()
            for k in range(1, half):
                to_owner(k).wait_send()

        return begin, pass_on, end, drain

    begin_a, pass_a, end_a, drain_a = reduction(across, gsend_a, gcore_a, grecv_a, ka_send, ka_recv, ga_send, ga_recv)
    begin_b, pass_b, end_b, drain_b = reduction(gram, gsend_b, gcore_b, grecv_b, kb_send, kb_recv, gb_send, gb_recv)
    t_across = to_x(total_out, total_in, t_send.at[0], t_recv.at[0])

    filter_chunk(0)
    begin_a()
    pairs(compose)
    pass_a()
    own_part()
    total_out[...] = end_a().astype(jnp.bfloat16)
    t_across.start()
    for copy in c_across[3:]:
        copy.start()
    filter_chunk(1)
    begin_b()
    pass_b()
    filter_chunk(2)
    total = end_b()
    t_across.wait_recv()
    total = (total + total_in[...].astype(jnp.float32)) * (1.0 / (2.0 * nbl * nb))

    high = total.astype(jnp.bfloat16)
    low = (total - high.astype(jnp.float32)).astype(jnp.bfloat16)
    basis_copy.wait()
    values = functions[...]
    image_g = jnp.dot(values, high, preferred_element_type=jnp.float32)
    image_g = image_g + jnp.dot(values, low, preferred_element_type=jnp.float32)
    product = image_g * values.astype(jnp.float32)
    top = product.astype(jnp.bfloat16)
    rest = (product - top.astype(jnp.float32)).astype(jnp.bfloat16)
    ones = jnp.ones((16, product.shape[1]), jnp.bfloat16)
    over_last = (((1,), (1,)), ((), ()))
    density = lax.dot_general(ones, top, over_last, preferred_element_type=jnp.float32)
    density = density + lax.dot_general(ones, rest, over_last, preferred_element_type=jnp.float32)
    dens_ref[...] = density[0:1]

    c_across[3].wait_recv()
    groups(far_first, 16)

    for copy in h_across + [n_across, t_across] + c_across[:4]:
        copy.wait_send()
    for when, copy in sent:
        when(copy.wait_send)
    drain_a()
    drain_b()
    c_across[4].wait_recv()
    groups(far_last, 16)
    c_across[4].wait_send()


def finish_kernel(filt_ref, dens_ref, filt_hbm, dens_hbm, sem):
    copies = [
        pltpu.make_async_copy(filt_ref, filt_hbm, sem.at[0]),
        pltpu.make_async_copy(dens_ref, dens_hbm, sem.at[1]),
    ]
    for copy in copies:
        copy.start()
    for copy in copies:
        copy.wait()


def plane_body(nb, coeffs, hamilton, neighbors, basis, occupation):
    elements, nbasis, nbl = coeffs.shape
    points = basis.shape[1]
    n = nbl // 5
    width = neighbors.shape[1]
    half = nb // 2
    dma = pltpu.SemaphoreType.DMA
    hbm = pl.BlockSpec(memory_space=pl.ANY)
    vmem = pl.BlockSpec(memory_space=pltpu.VMEM)
    nz = nb // 4
    forwards = 2 * (4 + 6 * (nz - 1) + 1 + 2 * (nz - 1))
    bf16, f32 = jnp.bfloat16, jnp.float32
    def chunk(rows, columns, dtype=bf16):
        return pltpu.VMEM((elements, rows, columns), dtype)

    rounds = [
        pltpu.VMEM((elements, nbasis, nbasis), bf16),
        pltpu.VMEM((half, nbasis, nbasis), bf16),
        pltpu.VMEM((half, nbasis, nbasis), bf16),
    ]
    operands = [coeffs, hamilton, neighbors.T, occupation.reshape(1, -1), basis]
    operands = [pltpu.with_memory_space_constraint(x, pltpu.HBM) for x in operands]
    filtered, density = pl.pallas_call(
        functools.partial(kernel, nb, n),
        out_shape=(
            jax.ShapeDtypeStruct(coeffs.shape, bf16),
            jax.ShapeDtypeStruct((1, points), f32),
        ),
        in_specs=[hbm] * 5,
        out_specs=(vmem, vmem),
        scratch_shapes=[
            chunk(nbasis, 2 * n), chunk(nbasis, n), chunk(nbasis, n),
            chunk(nbasis - nbasis // 4, n), chunk(nbasis // 4, n),
            chunk(nbasis, nbl), chunk(nbasis, nbl, f32),
            chunk(nbasis, 2 * n), chunk(nbasis, 2 * n),
            pltpu.VMEM((elements, 6, nbasis, nbasis), bf16),
            pltpu.VMEM((elements, 6, nbasis, nbasis), bf16),
            pltpu.VMEM((width, elements), jnp.int32),
            pltpu.SMEM((width, elements), jnp.int32),
            pltpu.SMEM((width, elements), jnp.int32),
            pltpu.VMEM((1, nbl), jnp.int32),
            pltpu.VMEM((points, nbasis), bf16),
            chunk(nbasis, nbasis, f32), chunk(nbasis, nbasis, f32),
            chunk(nbasis, 5 * (nbasis - nbasis // 4)), chunk(nbasis, 5 * (nbasis // 4)),
            chunk(nbasis, n, f32),
        ] + rounds + rounds + [
            pltpu.VMEM((nbasis, nbasis), bf16),
            pltpu.VMEM((nbasis, nbasis), bf16),
            dma((5,)), dma((5,)),
            dma((3,)), dma((3,)),
            dma((1,)), dma((1,)),
            dma((forwards,)), dma((2 * nb,)),
        ] + [dma((half,))] * 8 + [
            dma((1,)), dma((1,)),
            dma((1,)), dma((2,)), dma((4,)),
            pltpu.SemaphoreType.REGULAR, pltpu.SemaphoreType.REGULAR,
        ],
        compiler_params=pltpu.CompilerParams(
            collective_id=0, has_side_effects=True, vmem_limit_bytes=44 * 2**20),
    )(*operands)
    return pl.pallas_call(
        finish_kernel,
        out_shape=(
            jax.ShapeDtypeStruct(coeffs.shape, bf16),
            jax.ShapeDtypeStruct((1, points), f32),
        ),
        in_specs=[vmem, vmem],
        out_specs=(hbm, hbm),
        scratch_shapes=[dma((2,))],
        compiler_params=pltpu.CompilerParams(vmem_limit_bytes=8 * 2**20),
    )(filtered, density)


def solution(mesh):
    layers, nb = mesh.shape["layer"], mesh.shape["band"]

    def body(coeffs, hamilton, neighbors, basis, occupation):
        elements = coeffs.shape[0]
        one_kernel = (
            layers == 2 and elements == FY * FZ and nb == elements
            and nb % 4 == 0 and nb >= 8 and coeffs.shape[2] % 640 == 0
            and coeffs.shape[1] == 128 and basis.shape[0] == 1
        )
        if one_kernel:
            return plane_body(nb, coeffs, hamilton, neighbors, basis, occupation)
        return general_body(coeffs, hamilton, neighbors, basis, occupation)

    return jax.shard_map(
        body,
        mesh=mesh,
        in_specs=(
            P("layer", None, "band"),
            P("layer", None, None, None),
            P("layer", None),
            P(("layer", "band"), None, None),
            P(),
        ),
        out_specs=(P("layer", None, "band"), P(("layer", "band"), None)),
        check_vma=False,
    )
```

```python
import functools

import jax
import jax.numpy as jnp
from jax import lax
from jax.experimental import pallas as pl
from jax.experimental.pallas import tpu as pltpu
from jax.sharding import PartitionSpec as P

FY = 4
FZ = 4
MESH = pl.DeviceIdType.MESH

center = 0.5
half_width = 1.5


def with_halo(array, sides, width):
    for axis, dim in sides:
        devices, length = (lax.axis_size(axis), array.shape[dim])
        up = [(i, (i + 1) % devices) for i in range(devices - 1)]
        down = [(j, i) for i, j in up]
        last = lax.slice_in_dim(array, length - width, length, axis=dim)
        first = lax.slice_in_dim(array, 0, width, axis=dim)
        before = lax.ppermute(last, axis, up)
        after = lax.ppermute(first, axis, down)
        array = jnp.concatenate([before, array, after], axis=dim)
    return array


def neighbor_product(blocks, nearby):
    return jnp.einsum("ekij,ekjb->eib", blocks, nearby, preferred_element_type=jnp.float32)


def general_body(coeffs, hamilton, neighbors, basis, occupation):
    elements = coeffs.shape[0]
    face_size = FY * FZ
    offset = lax.axis_index("layer") * elements - face_size
    usable = neighbors >= 0
    position = jnp.where(usable, neighbors - offset, 0)
    allowed = usable.astype(jnp.bfloat16)

    def operate(source):
        padded = with_halo(source, (("layer", 0),), face_size)
        inside = source[position[:, :5] - face_size]
        result = neighbor_product(hamilton[:, :5], inside)
        across = padded[position[:, 5:]] * allowed[:, 5:, None, None]
        return result + neighbor_product(hamilton[:, 5:], across)

    start_vals = coeffs.astype(jnp.float32)
    first_image = operate(coeffs)
    filtered_once = ((first_image - center * start_vals) / half_width).astype(jnp.bfloat16)
    second_image = operate(filtered_once)
    filtered = (
        2.0 * (second_image - center * filtered_once.astype(jnp.float32)) / half_width - start_vals
    ).astype(jnp.bfloat16)
    weights = (1 + occupation).astype(jnp.float32) / (2.0 * occupation.shape[0])
    copies = lax.axis_size("band") // elements
    duplicated = jnp.tile(filtered, (copies, 1, 1))
    regrouped = lax.all_to_all(duplicated, "band", split_axis=0, concat_axis=2, tiled=True)
    orbital = jnp.dot(basis[0], regrouped[0], preferred_element_type=jnp.float32)
    density = jnp.sum(orbital * orbital * weights[None, :], axis=1)[None, :]
    return (filtered, density)


def kernel(nb, n, c_hbm, h_hbm, nbr_hbm, occ_hbm, basis_hbm, out_ref, dens_ref, *scratch):
    elements, nbasis, nbl = c_hbm.shape
    cx, cl = scratch[:3], scratch[3:5]
    (cown, ahead, f1o, f1x, hown, hx, nx_v, nown, nx, occ_v, functions, gram, across, row_a, row_b, base,
     gsend_a, gcore_a, grecv_a, gsend_b, gcore_b, grecv_b, total_out, total_in,
     c_send, c_recv, hx_send, hx_recv, n_send, n_recv, f_send, f_recv,
     ka_send, ka_recv, ga_send, ga_recv, kb_send, kb_recv, gb_send, gb_recv, t_send, t_recv,
     lc_sem, lh_sem, misc_sem, x_ready, all_in, hold, d_send, d_recv) = scratch[5:]
    layer, b = lax.axis_index("layer"), lax.axis_index("band")
    other = 1 - layer
    nz = nb // 4
    half = nb // 2
    site = b // 2
    z, y, core = b // 4, (b // 2) % 2, b % 2
    core_peer = b + 1 - 2 * core
    own_cross, x_cross = 6 - layer, 6 - other
    part = nbasis - nbasis // 4
    row_parts = (pl.ds(0, part), pl.ds(part, nbasis - part))
    widths = (2 * n, n, n, n)
    starts = (0, 2 * n, 3 * n, 4 * n)

    def ident(zz, yy, cc):
        return zz * 4 + yy * 2 + cc

    def place(s, side=layer):
        return pl.multiple_of(starts[s] + side * (nbl - widths[s] - 2 * starts[s]), n)

    barrier = pltpu.get_barrier_semaphore()

    @pl.when(layer == 0)
    def _():
        pl.semaphore_signal(barrier, inc=1, device_id={"layer": other, "band": b}, device_id_type=MESH)

    @pl.when(layer == 1)
    def _():
        pl.semaphore_wait(barrier, 1)
        pl.semaphore_signal(x_ready, inc=1, device_id={"layer": other, "band": b}, device_id_type=MESH)

    @pl.when(layer == 0)
    def _():
        pl.semaphore_wait(x_ready, 1)

    def to_x(src, dst, send, recv):
        return pltpu.make_async_remote_copy(
            src_ref=src, dst_ref=dst, send_sem=send, recv_sem=recv,
            device_id={"layer": other, "band": b}, device_id_type=MESH)

    def to_band(src, dst, send, recv, peer):
        return pltpu.make_async_remote_copy(
            src_ref=src, dst_ref=dst, send_sem=send, recv_sem=recv,
            device_id={"layer": layer, "band": peer}, device_id_type=MESH)

    pieces = ((0, 3), (3, 3))
    h_across = [
        to_x(h_hbm.at[b, pl.ds(0, 3)], hx.at[b, pl.ds(0, 3)], hx_send.at[0], hx_recv.at[0]),
        to_x(h_hbm.at[b, pl.ds(3, 2)], hx.at[b, pl.ds(3, 2)], hx_send.at[1], hx_recv.at[1]),
        to_x(h_hbm.at[b, pl.ds(own_cross, 1)], hx.at[b, pl.ds(5, 1)], hx_send.at[2], hx_recv.at[2]),
    ]
    n_across = to_x(nbr_hbm, nx_v, n_send.at[0], n_recv.at[0])
    c_across = [
        to_x(c_hbm.at[:, :, pl.ds(place(s, other), widths[s])], cx[s], c_send.at[s], c_recv.at[s]) for s in range(3)
    ] + [
        to_x(c_hbm.at[:, row_parts[i], pl.ds(place(3, other), n)], cl[i], c_send.at[3 + i], c_recv.at[3 + i])
        for i in range(2)
    ]
    eased = b < 2
    helps = jnp.logical_or(b == 2, b == 5)
    helped = jnp.maximum(b - 2, 0) // 3
    detour = to_x(h_hbm.at[helped, pl.ds(own_cross, 1)], hold, d_send.at[0], d_recv.at[0])
    relay = to_band(hold, hx.at[helped, pl.ds(5, 1)], d_send.at[1], hx_recv.at[2], helped)
    h_across[0].start()
    h_across[1].start()
    pl.when(jnp.logical_not(eased))(h_across[2].start)
    pl.when(helps)(detour.start)
    for copy in [n_across] + c_across[:3]:
        copy.start()

    n_copy = pltpu.make_async_copy(nbr_hbm, nown, misc_sem.at[0])
    occ_copy = pltpu.make_async_copy(occ_hbm.at[:, pl.ds(pl.multiple_of(b * nbl, n), nbl)], occ_v, misc_sem.at[2])
    basis_copy = pltpu.make_async_copy(basis_hbm.at[0], functions, misc_sem.at[3])
    h_copies = [
        pltpu.make_async_copy(h_hbm.at[:, pl.ds(0, 5)], hown.at[:, pl.ds(0, 5)], lh_sem.at[0]),
        pltpu.make_async_copy(h_hbm.at[:, pl.ds(own_cross, 1)], hown.at[:, pl.ds(5, 1)], lh_sem.at[1]),
    ]
    c_copy = pltpu.make_async_copy(c_hbm, cown, lc_sem.at[0])
    for copy in [n_copy, occ_copy, c_copy] + h_copies + [basis_copy]:
        copy.start()

    @pl.when(layer == 0)
    def _():
        for peer in [core_peer] + [(site + k) % half * 2 + core for k in range(1, half)]:
            pl.semaphore_signal(barrier, inc=1, device_id={"layer": layer, "band": peer}, device_id_type=MESH)
        pl.semaphore_wait(barrier, half)
        pl.semaphore_signal(all_in, inc=1, device_id={"layer": other, "band": b}, device_id_type=MESH)

    @pl.when(layer == 1)
    def _():
        pl.semaphore_wait(all_in, 1)

    def groups(body, size, low=0, high=elements):
        def several(t, carry):
            body([size * t + i for i in range(size)])
            return carry
        lax.fori_loop(low // size, high // size, several, 0)

    def pairs(body):
        groups(body, 2)

    for copy in [n_copy, c_copy] + h_copies:
        copy.wait()

    def in_plane(at):
        def one(e):
            row = jnp.concatenate([hown[e, k] for k in range(5)], axis=1)
            parts = jnp.concatenate([cown[lax.rem(nown[k, e], elements)] for k in range(5)], axis=0)
            return jnp.dot(row, parts, preferred_element_type=jnp.float32) - center * cown[e].astype(jnp.float32)
        for e, value in zip(at, [one(e) for e in at]):
            ahead[e] = value

    sent = []

    def always(body):
        body()

    def forward(block, i, peer, when=always):
        slot = len(sent)
        at, size = pieces[i]
        held = hx.at[block, pl.ds(at, size)]
        copy = to_band(held, held, f_send.at[slot], f_recv.at[block * 2 + i], peer)
        sent.append((when, copy))
        when(copy.start)

    def arrived(block, i, peer):
        at, size = pieces[i]
        held = hx.at[block, pl.ds(at, size)]
        to_band(held, held, f_send.at[0], f_recv.at[block * 2 + i], peer).wait_recv()

    def inside(zz):
        return pl.when(jnp.logical_and(zz >= 0, zz < nz))

    def both_inside(za, zb):
        return pl.when(jnp.logical_and(jnp.minimum(za, zb) >= 0, jnp.maximum(za, zb) < nz))

    y_peer = ident(z, 1 - y, core)
    groups(in_plane, 2, 0, 8)
    for i in range(2):
        h_across[i].wait_recv()
        if i == 1:
            h_across[2].wait_recv()
        for step in (1, -1):
            forward(b, i, ident(z + step, y, core), inside(z + step))
        forward(b, i, y_peer)
        forward(b, i, core_peer)

    @pl.when(helps)
    def _():
        detour.wait_recv()
        relay.start()

    groups(in_plane, 2, 8, elements)

    def over_y(away):
        for i in range(2):
            for step in (1, -1) if away else (1,):
                from_z = z - step * away
                block = ident(from_z, 1 - y, core)
                if away:
                    inside(from_z)(functools.partial(arrived, block, i, y_peer))
                    forward(block, i, core_peer, inside(from_z))
                else:
                    arrived(block, i, y_peer)
                    forward(block, i, core_peer)

    for away in range(1, nz):
        for i in range(2):
            for step in (1, -1):
                from_z = z - step * away
                block = ident(from_z, y, core)
                inside(from_z)(functools.partial(arrived, block, i, ident(z - step, y, core)))
                forward(block, i, ident(z + step, y, core), both_inside(from_z, z + step))
                forward(block, i, y_peer, inside(from_z))
                forward(block, i, core_peer, inside(from_z))
        over_y(away - 1)
    over_y(nz - 1)
    for zz in range(nz):
        for yy in range(2):
            for i in range(2):
                arrived(ident(zz, yy, 1 - core), i, core_peer)

    n_across.wait_recv()
    nx_copy = pltpu.make_async_copy(nx_v, nx, misc_sem.at[1])
    nx_copy.start()
    for copy in [nx_copy, occ_copy]:
        copy.wait()

    def image(blocks, table, e, cross, near, far):
        row = jnp.concatenate([blocks[e, k] for k in range(6)], axis=1)
        parts = [near(lax.rem(table[k, e], elements)) for k in range(5)]
        parts.append(far(lax.rem(table[cross, e], elements)))
        return jnp.dot(row, jnp.concatenate(parts, axis=0), preferred_element_type=jnp.float32)

    def once(got):
        return (got * (1.0 / half_width)).astype(jnp.bfloat16)

    def twice(got, middle, start):
        return (got - center * middle.astype(jnp.float32)) * (2.0 / half_width) - start.astype(jnp.float32)

    def square(value, weight):
        scaled = (value.astype(jnp.float32) * weight).astype(jnp.bfloat16)
        return lax.dot_general(scaled, value, (((1,), (1,)), ((), ())), preferred_element_type=jnp.float32)

    def filter_chunk(s):
        c_across[s].wait_recv()
        width = widths[s]
        columns = pl.ds(place(s), width)
        lanes = pl.ds(0, width)
        weight = (1 + occ_v[:, columns]).astype(jnp.float32)

        def own(e):
            return cown[e, :, columns]

        def far(e):
            return cx[s][e]

        def mine(e):
            return f1o[e, :, lanes]

        def theirs(e):
            return f1x[e, :, lanes]

        def first(at):
            across_x = [jnp.dot(hown[e, 5], far(lax.rem(nown[own_cross, e], elements)), preferred_element_type=jnp.float32)
                        for e in at]
            left = [once(ahead[e, :, columns] + got) for e, got in zip(at, across_x)]
            right = [once(image(hx, nx, e, x_cross, far, own) - center * far(e).astype(jnp.float32)) for e in at]
            for e, p, q in zip(at, left, right):
                f1o[e, :, lanes] = p
                f1x[e, :, lanes] = q

        def second(at):
            got = [twice(image(hown, nown, e, own_cross, mine, theirs), mine(e), own(e)).astype(jnp.bfloat16) for e in at]
            if s < 2:
                sums = [square(value, weight) for value in got]
                if s > 0:
                    sums = [added + gram[e] for e, added in zip(at, sums)]
                for e, added in zip(at, sums):
                    gram[e] = added
            for e, value in zip(at, got):
                out_ref[e, :, columns] = value

        def second_x(at):
            got = [twice(image(hx, nx, e, x_cross, theirs, mine), theirs(e), far(e)).astype(jnp.bfloat16) for e in at]
            for e, added in zip(at, [square(value, weight) for value in got]):
                across[e] = added

        size = 4
        groups(first, size)
        if s == 0:
            groups(second_x, size)
        groups(second, size)

    last_columns = pl.ds(place(3), n)

    def compose(at):
        def one(e, k):
            there = lax.rem(nown[own_cross, e], elements)
            beside = lax.rem(nown[k, e], elements)
            if k == 0:
                which = 0
            else:
                target = lax.rem(nown[own_cross, beside], elements)
                which = 0
                for j in range(1, 5):
                    which = jnp.where(lax.rem(nx[j, there], elements) == target, j, which)
            row = jnp.concatenate([hown[e, k], hown[e, 5]], axis=1)
            parts = jnp.concatenate([hown[beside, 5], hx[there, which]], axis=0)
            got = jnp.dot(row, parts, preferred_element_type=jnp.float32)
            if k == 0:
                got = got - (2.0 * center) * hown[e, 5].astype(jnp.float32)
            return (got * (2.0 / half_width / half_width)).astype(jnp.bfloat16)
        rows = [[one(e, k) for k in range(5)] for e in at]
        for e, row in zip(at, rows):
            row_a[e] = jnp.concatenate([block[:, :part] for block in row], axis=1)
            row_b[e] = jnp.concatenate([block[:, part:] for block in row], axis=1)

    def own_part():
        def own(e):
            return cown[e, :, last_columns]

        def mine(e):
            return f1o[e, :, pl.ds(0, n)]

        def theirs(e):
            return f1x[e, :, pl.ds(0, n)]

        def first(at):
            left = [once(ahead[e, :, last_columns]) for e in at]
            right = [once(jnp.dot(hx[e, 5], own(lax.rem(nx[x_cross, e], elements)), preferred_element_type=jnp.float32))
                     for e in at]
            for e, p, q in zip(at, left, right):
                f1o[e, :, pl.ds(0, n)] = p
                f1x[e, :, pl.ds(0, n)] = q

        def second(at):
            got = [twice(image(hown, nown, e, own_cross, mine, theirs), mine(e), own(e)) for e in at]
            for e, value in zip(at, got):
                base[e] = value

        groups(first, 4)
        groups(second, 4)

    def far_part(row, held, e):
        parts = [held[lax.rem(nown[own_cross, lax.rem(nown[k, e], elements)], elements)] for k in range(5)]
        return base[e] + jnp.dot(row[e], jnp.concatenate(parts, axis=0), preferred_element_type=jnp.float32)

    def far_first(at):
        for e, value in zip(at, [far_part(row_a, cl[0], e) for e in at]):
            base[e] = value

    def far_last(at):
        for e, value in zip(at, [far_part(row_b, cl[1], e) for e in at]):
            out_ref[e, :, last_columns] = value.astype(jnp.bfloat16)

    def reduction(source, gsend, gcore, grecv, k_send, k_recv, g_send, g_recv):
        def to_core(t):
            return to_band(gsend.at[2 * t + 1 - core], gcore.at[t], k_send.at[t], k_recv.at[t], core_peer)

        def to_owner(k):
            element = (site + k) % half * 2 + core
            return to_band(gsend.at[element], grecv.at[k], g_send.at[k], g_recv.at[k], element)

        def pair_up(t, carry):
            gsend[2 * t + 1 - core] = source[2 * t + 1 - core].astype(jnp.bfloat16)
            to_core(t).start()
            return carry

        def hand_over(i, carry):
            k = i + 1
            t = (site + k) % half
            to_core(t).wait_recv()
            gsend[2 * t + core] = (source[2 * t + core] + gcore[t].astype(jnp.float32)).astype(jnp.bfloat16)
            to_owner(k).start()
            return carry

        def begin():
            lax.fori_loop(0, half, pair_up, 0)

        def pass_on():
            lax.fori_loop(0, half - 1, hand_over, 0)

        def end():
            to_core(site).wait_recv()
            total = source[b] + gcore[site].astype(jnp.float32)
            for k in range(1, half):
                to_owner(k).wait_recv()
                total = total + grecv[k].astype(jnp.float32)
            return total

        def drain():
            for t in range(half):
                to_core(t).wait_send()
            for k in range(1, half):
                to_owner(k).wait_send()

        return begin, pass_on, end, drain

    begin_a, pass_a, end_a, drain_a = reduction(across, gsend_a, gcore_a, grecv_a, ka_send, ka_recv, ga_send, ga_recv)
    begin_b, pass_b, end_b, drain_b = reduction(gram, gsend_b, gcore_b, grecv_b, kb_send, kb_recv, gb_send, gb_recv)
    t_across = to_x(total_out, total_in, t_send.at[0], t_recv.at[0])

    filter_chunk(0)
    begin_a()
    pairs(compose)
    pass_a()
    own_part()
    total_out[...] = end_a().astype(jnp.bfloat16)
    t_across.start()
    for copy in c_across[3:]:
        copy.start()
    filter_chunk(1)
    begin_b()
    pass_b()
    filter_chunk(2)
    total = end_b()
    t_across.wait_recv()
    total = (total + total_in[...].astype(jnp.float32)) * (1.0 / (2.0 * nbl * nb))

    high = total.astype(jnp.bfloat16)
    low = (total - high.astype(jnp.float32)).astype(jnp.bfloat16)
    basis_copy.wait()
    values = functions[...]
    image_g = jnp.dot(values, high, preferred_element_type=jnp.float32)
    image_g = image_g + jnp.dot(values, low, preferred_element_type=jnp.float32)
    product = image_g * values.astype(jnp.float32)
    top = product.astype(jnp.bfloat16)
    rest = (product - top.astype(jnp.float32)).astype(jnp.bfloat16)
    ones = jnp.ones((16, product.shape[1]), jnp.bfloat16)
    over_last = (((1,), (1,)), ((), ()))
    density = lax.dot_general(ones, top, over_last, preferred_element_type=jnp.float32)
    density = density + lax.dot_general(ones, rest, over_last, preferred_element_type=jnp.float32)
    dens_ref[...] = density[0:1]

    c_across[3].wait_recv()
    groups(far_first, 16)

    pl.when(jnp.logical_not(eased))(h_across[2].wait_send)
    pl.when(helps)(detour.wait_send)
    pl.when(helps)(relay.wait_send)
    for copy in [h_across[0], h_across[1], n_across, t_across] + c_across[:4]:
        copy.wait_send()
    for when, copy in sent:
        when(copy.wait_send)
    drain_a()
    drain_b()
    c_across[4].wait_recv()
    groups(far_last, 16)
    c_across[4].wait_send()


def finish_kernel(filt_ref, dens_ref, filt_hbm, dens_hbm, sem):
    copies = [
        pltpu.make_async_copy(filt_ref, filt_hbm, sem.at[0]),
        pltpu.make_async_copy(dens_ref, dens_hbm, sem.at[1]),
    ]
    for copy in copies:
        copy.start()
    for copy in copies:
        copy.wait()


def plane_body(nb, coeffs, hamilton, neighbors, basis, occupation):
    elements, nbasis, nbl = coeffs.shape
    points = basis.shape[1]
    n = nbl // 5
    width = neighbors.shape[1]
    half = nb // 2
    dma = pltpu.SemaphoreType.DMA
    hbm = pl.BlockSpec(memory_space=pl.ANY)
    vmem = pl.BlockSpec(memory_space=pltpu.VMEM)
    nz = nb // 4
    forwards = 2 * (4 + 6 * (nz - 1) + 1 + 2 * (nz - 1))
    bf16, f32 = jnp.bfloat16, jnp.float32
    def chunk(rows, columns, dtype=bf16):
        return pltpu.VMEM((elements, rows, columns), dtype)

    rounds = [
        pltpu.VMEM((elements, nbasis, nbasis), bf16),
        pltpu.VMEM((half, nbasis, nbasis), bf16),
        pltpu.VMEM((half, nbasis, nbasis), bf16),
    ]
    operands = [coeffs, hamilton, neighbors.T, occupation.reshape(1, -1), basis]
    operands = [pltpu.with_memory_space_constraint(x, pltpu.HBM) for x in operands]
    filtered, density = pl.pallas_call(
        functools.partial(kernel, nb, n),
        out_shape=(
            jax.ShapeDtypeStruct(coeffs.shape, bf16),
            jax.ShapeDtypeStruct((1, points), f32),
        ),
        in_specs=[hbm] * 5,
        out_specs=(vmem, vmem),
        scratch_shapes=[
            chunk(nbasis, 2 * n), chunk(nbasis, n), chunk(nbasis, n),
            chunk(nbasis - nbasis // 4, n), chunk(nbasis // 4, n),
            chunk(nbasis, nbl), chunk(nbasis, nbl, f32),
            chunk(nbasis, 2 * n), chunk(nbasis, 2 * n),
            pltpu.VMEM((elements, 6, nbasis, nbasis), bf16),
            pltpu.VMEM((elements, 6, nbasis, nbasis), bf16),
            pltpu.VMEM((width, elements), jnp.int32),
            pltpu.SMEM((width, elements), jnp.int32),
            pltpu.SMEM((width, elements), jnp.int32),
            pltpu.VMEM((1, nbl), jnp.int32),
            pltpu.VMEM((points, nbasis), bf16),
            chunk(nbasis, nbasis, f32), chunk(nbasis, nbasis, f32),
            chunk(nbasis, 5 * (nbasis - nbasis // 4)), chunk(nbasis, 5 * (nbasis // 4)),
            chunk(nbasis, n, f32),
        ] + rounds + rounds + [
            pltpu.VMEM((nbasis, nbasis), bf16),
            pltpu.VMEM((nbasis, nbasis), bf16),
            dma((5,)), dma((5,)),
            dma((3,)), dma((3,)),
            dma((1,)), dma((1,)),
            dma((forwards,)), dma((2 * nb,)),
        ] + [dma((half,))] * 8 + [
            dma((1,)), dma((1,)),
            dma((1,)), dma((2,)), dma((4,)),
            pltpu.SemaphoreType.REGULAR, pltpu.SemaphoreType.REGULAR,
            pltpu.VMEM((1, nbasis, nbasis), bf16), dma((2,)), dma((1,)),
        ],
        compiler_params=pltpu.CompilerParams(
            collective_id=0, has_side_effects=True, vmem_limit_bytes=44 * 2**20),
    )(*operands)
    return pl.pallas_call(
        finish_kernel,
        out_shape=(
            jax.ShapeDtypeStruct(coeffs.shape, bf16),
            jax.ShapeDtypeStruct((1, points), f32),
        ),
        in_specs=[vmem, vmem],
        out_specs=(hbm, hbm),
        scratch_shapes=[dma((2,))],
        compiler_params=pltpu.CompilerParams(vmem_limit_bytes=8 * 2**20),
    )(filtered, density)


def solution(mesh):
    layers, nb = mesh.shape["layer"], mesh.shape["band"]

    def body(coeffs, hamilton, neighbors, basis, occupation):
        elements = coeffs.shape[0]
        one_kernel = (
            layers == 2 and elements == FY * FZ and nb == elements
            and nb % 4 == 0 and nb >= 8 and coeffs.shape[2] % 640 == 0
            and coeffs.shape[1] == 128 and basis.shape[0] == 1
        )
        if one_kernel:
            return plane_body(nb, coeffs, hamilton, neighbors, basis, occupation)
        return general_body(coeffs, hamilton, neighbors, basis, occupation)

    return jax.shard_map(
        body,
        mesh=mesh,
        in_specs=(
            P("layer", None, "band"),
            P("layer", None, None, None),
            P("layer", None),
            P(("layer", "band"), None, None),
            P(),
        ),
        out_specs=(P("layer", None, "band"), P(("layer", "band"), None)),
        check_vma=False,
    )
```
